256 devices in a mesh: ctx: 4 (over y), ch: 64 (over z, x, core).
Axes of the slice: x: 4, y: 4, z: 8, core: 2. Of those that a mesh axis runs over, the one named last changes fastest.
Arguments:
- query_gate: bfloat16 [4096, 8192], P('ch', 'ctx'), may hold values from -6 to 6
- key_gate: bfloat16 [4096, 8192], P('ch', 'ctx'), may hold values from -6 to 6
- value_proj: bfloat16 [4096, 8192], P('ch', 'ctx'), may hold values from -6 to 6
- filter_taps: bfloat16 [4096, 8192], P('ch'), may hold values from -0.0625 to 0.0625
- out_weight: bfloat16 [4096, 4096], P(None, 'ch'), may hold values from -0.09375 to 0.09375
Outputs:
- layer_out: bfloat16 [4096, 8192], P('ch', 'ctx')
The draws below stay inside these ranges and needn't reach their ends.
All inputs are finite; a program needn't handle non-finite values.
Results may differ from the reference program's by a relative error of at most 0.015.
Values may be sent and summed in bfloat16 or wider, within the bound.
A program may use at most 128 MiB of HBM per device.

```python
import jax
import jax.numpy as jnp
from jax import lax

D = 4096
SEQ = 8192


def shard_levels(rng, dims, cuts, least, top_value):
    level = 1.0
    for position, blocks in cuts:
        draws = jax.random.uniform(jax.random.fold_in(jax.random.fold_in(rng, 6), position), (blocks,), jnp.float32, least / len(cuts), top_value / len(cuts))
        level = level * jnp.repeat(jnp.exp(draws), dims[position] // blocks).reshape((-1,) + (1,) * (len(dims) - 1 - position))
    return level


def centred(own_key, shape, spread, reach, split=(), kind=jnp.bfloat16):
    entries = spread * jax.random.normal(own_key, shape, jnp.float32)
    if split:
        entries = entries * shard_levels(own_key, shape, split, -0.22, 0.18)
    return jnp.clip(entries, -reach, reach).astype(kind)


def setup_inputs(seed: int = 0) -> dict:
    seeds = jax.random.split(jax.random.key(seed), 6)
    return {
        "query_gate": centred(seeds[0], (D, SEQ), 1.0, 6.0, ((0, 64), (1, 4))),
        "key_gate": centred(seeds[1], (D, SEQ), 1.0, 6.0, ((0, 64), (1, 4))),
        "value_proj": centred(seeds[2], (D, SEQ), 1.0, 6.0, ((0, 64), (1, 4))),
        "filter_taps": centred(seeds[3], (D, SEQ), SEQ ** -0.5, 0.0625, ((0, 64),)),
        "out_weight": centred(seeds[4], (D, D), D ** -0.5, 0.09375, ((1, 64),)),
    }


def reference(query_gate, key_gate, value_proj, filter_taps, out_weight):
    rounded = (key_gate.astype(jnp.float32) * value_proj.astype(jnp.float32)).astype(jnp.bfloat16)
    product = lax.optimization_barrier(rounded).astype(jnp.float32)
    fft_length = 2 * SEQ
    spectrum = jnp.fft.rfft(product, n=fft_length, axis=1) * jnp.fft.rfft(filter_taps.astype(jnp.float32), n=fft_length, axis=1)
    convolved = jnp.fft.irfft(spectrum, n=fft_length, axis=1)[:, :SEQ].astype(jnp.float32)
    gated = (query_gate.astype(jnp.float32) * convolved).astype(jnp.bfloat16)
    layer_out = lax.dot_general(out_weight, gated, (((0,), (0,)), ((), ())), preferred_element_type=jnp.float32)
    return layer_out.astype(jnp.bfloat16)
```

```python
import jax
import jax.numpy as jnp
import ml_dtypes
import numpy as np
from jax import lax
from jax.experimental import pallas as pl
from jax.experimental.pallas import tpu as pltpu
from jax.sharding import PartitionSpec as P

SEQ = 8192
N1 = 64
N2 = 128
CTX = 4
GROUP = 8
CHAN = 16
BATCH = 4

bf16 = jnp.bfloat16
f32 = jnp.float32


def two_parts(table):
    high = table.astype(ml_dtypes.bfloat16)
    low = (table - high.astype(np.float64)).astype(ml_dtypes.bfloat16)
    return high, low


def tables():
    root = np.pi / (2 * SEQ)
    n1, k1, n2, k2 = np.arange(N1), np.arange(N1), np.arange(N2), np.arange(N2)
    first = np.exp(1j * (root * N2 * n1[None, :] - 2 * np.pi * k1[:, None] * n1[None, :] / N1))
    twist = np.exp(1j * (root * n2[None, :] - 2 * np.pi * k1[:, None] * n2[None, :] / SEQ))
    second = np.exp(-2j * np.pi * n2[:, None] * k2[None, :] / N2)
    high, low = two_parts(np.concatenate([first.real, first.imag], axis=0))
    stage1 = np.concatenate([high, low], axis=1)
    fwd = two_parts(np.block([[second.real, second.imag], [-second.imag, second.real]]))
    inv = two_parts(np.block([[second.real, -second.imag], [second.imag, second.real]]))
    high, low = two_parts(np.concatenate([first.real.T, first.imag.T], axis=1) / SEQ)
    last = np.concatenate([high, low], axis=1)
    twist2 = np.concatenate([twist.real, twist.imag], axis=1).astype(np.float32)
    return stage1, np.stack(fwd), np.stack(inv), last, twist2


def dot(a, b):
    return jnp.dot(a, b, preferred_element_type=f32)


def parts_of(x):
    high = x.astype(bf16)
    return high, (x - high.astype(f32)).astype(bf16)


def dot3(x, table_ref):
    high, low = parts_of(x)
    return dot(high, table_ref[0]) + (dot(low, table_ref[0]) + dot(high, table_ref[1]))


def convolve(sig, filt, conv, stage1_ref, fwd_ref, inv_ref, last_ref, twist_ref):
    stage1 = stage1_ref[...]
    tw_re, tw_im = twist_ref[:, :N2], twist_ref[:, N2:]

    def spectrum(ref, c0):
        rows = []
        for c in range(BATCH):
            x = ref[pl.ds(c0 + c, N1, stride=CHAN), :].astype(bf16)
            a = dot(stage1, jnp.concatenate([x, x], axis=0))
            re, im = a[:N1], a[N1:]
            rows.append(
                jnp.concatenate([re * tw_re - im * tw_im, re * tw_im + im * tw_re], axis=1)
            )
        return dot3(jnp.concatenate(rows, axis=0), fwd_ref)

    def step(i, _):
        c0 = i * BATCH
        fs = spectrum(filt, c0)
        ss = spectrum(sig, c0)
        fr, fi, sr, si = fs[:, :N2], fs[:, N2:], ss[:, :N2], ss[:, N2:]
        prod = jnp.concatenate([fr * sr - fi * si, fr * si + fi * sr], axis=1)
        back = dot3(prod, inv_ref)
        last = last_ref[...]
        for c in range(BATCH):
            re = back[c * N1 : (c + 1) * N1, :N2]
            im = back[c * N1 : (c + 1) * N1, N2:]
            u = jnp.concatenate([re * tw_re + im * tw_im, im * tw_re - re * tw_im], axis=0)
            high, low = parts_of(u)
            y = dot(last, jnp.concatenate([high, high], axis=0)) + dot(last[:, :N2], low)
            conv[pl.ds(c0 + c, N1, stride=CHAN), :] = y
        return 0

    lax.fori_loop(0, CHAN // BATCH, step, 0)


def conv_kernel(p_ref, q_ref, f_ref, s1, fw, iv, la, tw, out_ref, sig, filt, conv):
    for n in range(N1):
        cols = slice(n * N2, (n + 1) * N2)
        sig[n * CHAN : (n + 1) * CHAN, :] = p_ref[:, cols].astype(f32)
        filt[n * CHAN : (n + 1) * CHAN, :] = f_ref[:, cols].astype(f32)
    convolve(sig, filt, conv, s1, fw, iv, la, tw)
    for n in range(N1):
        cols = slice(n * N2, (n + 1) * N2)
        out_ref[:, cols] = (
            q_ref[:, cols].astype(f32) * conv[n * CHAN : (n + 1) * CHAN, :]
        ).astype(bf16)


def gated_convolution(p, q, f):
    return pl.pallas_call(
        conv_kernel,
        out_shape=jax.ShapeDtypeStruct((CHAN, SEQ), bf16),
        scratch_shapes=[pltpu.VMEM((N1 * CHAN, N2), f32)] * 3,
        compiler_params=pltpu.CompilerParams(vmem_limit_bytes=32 * 1024 * 1024),
    )(p, q, f, *[jnp.asarray(t) for t in tables()])


def per_device(query_gate, key_gate, value_proj, filter_taps, out_weight):
    same_z = [[z * GROUP + j for j in range(GROUP)] for z in range(8)]
    same_j = [[z * GROUP + j for z in range(8)] for j in range(GROUP)]
    slab = lax.all_gather(out_weight.T, "ch", axis=0, tiled=True, axis_index_groups=same_z)
    product = (key_gate.astype(f32) * value_proj.astype(f32)).astype(bf16)
    both = jnp.stack([product, query_gate])
    both = lax.all_to_all(both, "ctx", split_axis=1, concat_axis=2, tiled=True)
    own = lax.axis_index("ctx") * CHAN
    taps = lax.dynamic_slice(filter_taps, (own, 0), (CHAN, SEQ))
    gated = gated_convolution(both[0], both[1], taps)
    gated = lax.all_to_all(gated, "ctx", split_axis=1, concat_axis=0, tiled=True)
    gated = lax.all_to_all(
        gated, "ch", split_axis=1, concat_axis=0, tiled=True, axis_index_groups=same_z
    )
    gated = lax.all_gather(gated, "ch", axis=0, tiled=True, axis_index_groups=same_j)
    out = jnp.dot(slab, gated, preferred_element_type=f32).astype(bf16)
    return lax.all_to_all(
        out, "ch", split_axis=0, concat_axis=1, tiled=True, axis_index_groups=same_z
    )


def solution(mesh):
    return jax.shard_map(
        per_device,
        mesh=mesh,
        in_specs=(P("ch", "ctx"), P("ch", "ctx"), P("ch", "ctx"), P("ch", None), P(None, "ch")),
        out_specs=P("ch", "ctx"),
        check_vma=False,
    )
```

```python
import jax
import jax.numpy as jnp
import ml_dtypes
import numpy as np
from jax import lax
from jax.experimental import pallas as pl
from jax.experimental.pallas import tpu as pltpu
from jax.sharding import PartitionSpec as P

SEQ = 8192
N1 = 64
N2 = 128
CTX = 4
GROUP = 8
CHAN = 16
BATCH = 4
RING = 8
PLANE = CTX * GROUP
TOK = 256
D = 4096
SLAB = D // RING
MESH = pl.DeviceIdType.MESH

bf16 = jnp.bfloat16
f32 = jnp.float32


def two_parts(table):
    high = table.astype(ml_dtypes.bfloat16)
    low = (table - high.astype(np.float64)).astype(ml_dtypes.bfloat16)
    return high, low


def tables():
    root = np.pi / (2 * SEQ)
    n1, k1, n2, k2 = np.arange(N1), np.arange(N1), np.arange(N2), np.arange(N2)
    first = np.exp(1j * (root * N2 * n1[None, :] - 2 * np.pi * k1[:, None] * n1[None, :] / N1))
    twist = np.exp(1j * (root * n2[None, :] - 2 * np.pi * k1[:, None] * n2[None, :] / SEQ))
    second = np.exp(-2j * np.pi * n2[:, None] * k2[None, :] / N2)
    high, low = two_parts(np.concatenate([first.real, first.imag], axis=0))
    stage1 = np.concatenate([high, low], axis=1)
    fwd = two_parts(np.block([[second.real, second.imag], [-second.imag, second.real]]))
    inv = two_parts(np.block([[second.real, -second.imag], [second.imag, second.real]]))
    high, low = two_parts(np.concatenate([first.real.T, first.imag.T], axis=1) / SEQ)
    last = np.concatenate([high, low], axis=1)
    twist2 = np.concatenate([twist.real, twist.imag], axis=1).astype(np.float32)
    return stage1, np.stack(fwd), np.stack(inv), last, twist2


def dot(a, b):
    return jnp.dot(a, b, preferred_element_type=f32)


def parts_of(x):
    high = x.astype(bf16)
    return high, (x - high.astype(f32)).astype(bf16)


def dot3(x, table_ref):
    high, low = parts_of(x)
    return dot(high, table_ref[0]) + (dot(low, table_ref[0]) + dot(high, table_ref[1]))


def spectrum(ref, c0, stage1, tw_re, tw_im, fwd_ref):
    rows = []
    for c in range(BATCH):
        x = ref[pl.ds(c0 + c, N1, stride=CHAN), :].astype(bf16)
        a = dot(stage1, jnp.concatenate([x, x], axis=0))
        re, im = a[:N1], a[N1:]
        rows.append(jnp.concatenate([re * tw_re - im * tw_im, re * tw_im + im * tw_re], axis=1))
    return dot3(jnp.concatenate(rows, axis=0), fwd_ref)


def layer_kernel(
    q_ref, k_ref, v_ref, f_ref, w_ref, s1_ref, fwd_ref, inv_ref, last_ref, tw_ref,
    out_ref,
    prod, pbuf, qbuf, sig, filt, conv, fspec, gsend, gbuf, wbuf, acc, osend, obuf,
    p_send, p_recv, q_send, q_recv, w_send, w_recv, s_send, s_recv,
    g_send, g_recv, r_send, r_recv, l_send, l_recv, o_send, o_recv,
):
    ctx = lax.axis_index("ctx")
    ch = lax.axis_index("ch")
    z, j = ch // GROUP, ch % GROUP
    x, core = j // 2, j % 2
    me = ctx * GROUP + j

    def at(other_ctx, other_z, other_j):
        return (other_ctx, other_z * GROUP + other_j)

    def send(src, dst, send_sem, recv_sem, device):
        copy = pltpu.make_async_remote_copy(
            src_ref=src, dst_ref=dst, send_sem=send_sem, recv_sem=recv_sem,
            device_id=device, device_id_type=MESH,
        )
        copy.start()
        return copy

    up, down = at(ctx, (z + 1) % RING, j), at(ctx, (z + RING - 1) % RING, j)
    barrier = pltpu.get_barrier_semaphore()

    def greet(i, _):
        peer = (me + 1 + i) % PLANE
        pl.semaphore_signal(
            barrier, inc=1, device_id=at(peer // GROUP, z, peer % GROUP), device_id_type=MESH
        )
        return 0

    lax.fori_loop(0, PLANE - 1, greet, 0)
    pl.semaphore_signal(barrier, inc=1, device_id=up, device_id_type=MESH)
    pl.semaphore_signal(barrier, inc=1, device_id=down, device_id_type=MESH)

    prod[...] = (k_ref[...].astype(f32) * v_ref[...].astype(f32)).astype(bf16)
    pl.semaphore_wait(barrier, PLANE + 1)

    waits = []
    for refs in ((prod, pbuf, p_send, p_recv), (q_ref, qbuf, q_send, q_recv)):
        src, dst, send_sem, recv_sem = refs
        for i in range(1, CTX):
            peer = (ctx + i) % CTX
            waits.append(
                send(src.at[peer], dst.at[ctx], send_sem.at[i], recv_sem.at[i], at(peer, z, j))
            )
    p_waits, q_waits = waits[: CTX - 1], waits[CTX - 1 :]
    pbuf[ctx] = prod[ctx]
    qbuf[ctx] = q_ref[ctx]

    def turn(i, _):
        rows = pl.ds(pl.multiple_of(i * 128, 128), 128)
        wbuf[j, :, rows] = w_ref[rows, :].astype(f32).T.astype(bf16)
        return 0

    lax.fori_loop(0, D // 128, turn, 0)
    xr, xl = (x + 1) % 4, (x + 3) % 4
    right, left = at(ctx, z, xr * 2 + core), at(ctx, z, xl * 2 + core)
    sibling = at(ctx, z, x * 2 + 1 - core)
    j_right, j_left, j_far = xr * 2 + core, xl * 2 + core, ((x + 2) % 4) * 2 + core
    w_waits = [
        send(wbuf.at[j], wbuf.at[j], w_send.at[0], w_recv.at[0], right),
        send(wbuf.at[j], wbuf.at[j], w_send.at[1], w_recv.at[1], left),
    ]
    s_waits = [send(wbuf.at[j], wbuf.at[j], s_send.at[0], s_recv.at[0], sibling)]

    own = pl.ds(pl.multiple_of(ctx * CHAN, CHAN), CHAN)
    for n in range(N1):
        filt[n * CHAN : (n + 1) * CHAN, :] = f_ref[own, n * N2 : (n + 1) * N2].astype(f32)
    stage1 = s1_ref[...]
    tw_re, tw_im = tw_ref[:, :N2], tw_ref[:, N2:]

    def filter_step(i, _):
        fspec[i] = spectrum(filt, i * BATCH, stage1, tw_re, tw_im, fwd_ref)
        return 0

    lax.fori_loop(0, CHAN // BATCH, filter_step, 0)

    for copy in p_waits:
        copy.wait_recv()
    for n in range(N1):
        col = (n % 16) * N2
        sig[n * CHAN : (n + 1) * CHAN, :] = pbuf[n // 16, :, col : col + N2].astype(f32)

    def conv_step(i, _):
        c0 = i * BATCH
        fs = fspec[i]
        ss = spectrum(sig, c0, stage1, tw_re, tw_im, fwd_ref)
        fr, fi, sr, si = fs[:, :N2], fs[:, N2:], ss[:, :N2], ss[:, N2:]
        back = dot3(jnp.concatenate([fr * sr - fi * si, fr * si + fi * sr], axis=1), inv_ref)
        last = last_ref[...]
        for c in range(BATCH):
            re = back[c * N1 : (c + 1) * N1, :N2]
            im = back[c * N1 : (c + 1) * N1, N2:]
            u = jnp.concatenate([re * tw_re + im * tw_im, im * tw_re - re * tw_im], axis=0)
            high, low = parts_of(u)
            y = dot(last, jnp.concatenate([high, high], axis=0)) + dot(last[:, :N2], low)
            conv[pl.ds(c0 + c, N1, stride=CHAN), :] = y
        return 0

    lax.fori_loop(0, CHAN // BATCH, conv_step, 0)

    for copy in q_waits:
        copy.wait_recv()
    for n in range(N1):
        col = (n % 16) * N2
        gate = qbuf[n // 16, :, col : col + N2].astype(f32)
        gsend[n // 2, :, (n % 2) * N2 : (n % 2 + 1) * N2] = (
            gate * conv[n * CHAN : (n + 1) * CHAN, :]
        ).astype(bf16)

    slot = j * CTX + ctx

    def tile_copy(i):
        peer = (me + i) % PLANE
        return pltpu.make_async_remote_copy(
            src_ref=gsend.at[peer], dst_ref=gbuf.at[z, slot], send_sem=g_send.at[i],
            recv_sem=g_recv.at[slot], device_id=at(peer // GROUP, z, peer % GROUP),
            device_id_type=MESH,
        )

    def scatter(i, _):
        tile_copy(i).start()
        return 0

    lax.fori_loop(1, PLANE, scatter, 0)
    gbuf[z, slot] = gsend[me]

    def arrived(i, _):
        @pl.when(i != slot)
        def _():
            pltpu.make_async_remote_copy(
                src_ref=gsend.at[0], dst_ref=gbuf.at[z, i], send_sem=g_send.at[0],
                recv_sem=g_recv.at[i], device_id=up, device_id_type=MESH,
            ).wait_recv()

        return 0

    half = PLANE // 2

    def pass_on(step, h):
        rows = pl.ds(h * half, half)
        up_slab, down_slab = (z + RING - step) % RING, (z + step) % RING
        ups = downs = None
        if step < 3 or h == 0:
            part = gbuf.at[up_slab, rows]
            ups = send(part, part, r_send.at[step, h], r_recv.at[step, h], up)
        if step < 3 or h == 1:
            part = gbuf.at[down_slab, rows]
            downs = send(part, part, l_send.at[step, h], l_recv.at[step, h], down)
        return ups, downs

    hops = {}
    for h in range(2):
        lax.fori_loop(h * half, (h + 1) * half, arrived, 0)
        hops[0, h] = pass_on(0, h)

    w_waits[0].wait_recv()
    part = wbuf.at[j_left, pl.ds(0, 32)]
    w_waits.append(send(part, part, w_send.at[2], w_recv.at[2], right))
    part = wbuf.at[j_left]
    s_waits.append(send(part, part, s_send.at[1], s_recv.at[1], sibling))
    w_waits[1].wait_recv()
    part = wbuf.at[j_right, pl.ds(32, 32)]
    w_waits.append(send(part, part, w_send.at[3], w_recv.at[3], left))
    part = wbuf.at[j_right]
    s_waits.append(send(part, part, s_send.at[2], s_recv.at[2], sibling))

    def take(step):
        for h in range(2):
            ups, downs = hops[step, h]
            if ups is not None:
                ups.wait_recv()
            if downs is not None:
                downs.wait_recv()
            if step < 3:
                hops[step + 1, h] = pass_on(step + 1, h)

    def project(offset, first=False):
        slab = (z + offset) % RING
        cols = pl.ds(pl.multiple_of(slab * SLAB, SLAB), SLAB)
        weight = wbuf[:, :, cols].reshape(SLAB, SLAB)
        term = dot(weight, gbuf[slab].reshape(SLAB, TOK))
        acc[...] = term if first else acc[...] + term

    take(0)
    w_waits[2].wait_recv()
    w_waits[3].wait_recv()
    part = wbuf.at[j_far]
    s_waits.append(send(part, part, s_send.at[3], s_recv.at[3], sibling))
    take(1)
    for copy in s_waits:
        copy.wait_recv()
    project(0, first=True)
    project(1)
    project(RING - 1)
    take(2)
    project(2)
    project(RING - 2)
    project(3)
    project(RING - 3)
    take(3)
    project(4)

    osend[...] = acc[...].reshape(GROUP, 64, TOK).astype(bf16)
    o_waits = []
    for i in range(1, GROUP):
        peer = (j + i) % GROUP
        o_waits.append(
            send(osend.at[peer], obuf.at[j], o_send.at[i], o_recv.at[i], at(ctx, z, peer))
        )
    obuf[j] = osend[j]
    for copy in o_waits:
        copy.wait_recv()
    for i in range(GROUP):
        out_ref[:, i * TOK : (i + 1) * TOK] = obuf[i]

    for copy in p_waits + q_waits + w_waits + s_waits + o_waits:
        copy.wait_send()
    for ups, downs in hops.values():
        if ups is not None:
            ups.wait_send()
        if downs is not None:
            downs.wait_send()

    def sent(i, _):
        tile_copy(i).wait_send()
        return 0

    lax.fori_loop(1, PLANE, sent, 0)


def per_device(query_gate, key_gate, value_proj, filter_taps, out_weight):
    tokens = SEQ // CTX
    split = (CTX, CHAN, tokens)
    dma = pltpu.SemaphoreType.DMA
    return pl.pallas_call(
        layer_kernel,
        out_shape=jax.ShapeDtypeStruct((CTX * CHAN, tokens), bf16),
        in_specs=[pl.BlockSpec(memory_space=pltpu.VMEM)] * 10,
        out_specs=pl.BlockSpec(memory_space=pltpu.VMEM),
        scratch_shapes=[
            pltpu.VMEM(split, bf16),
            pltpu.VMEM(split, bf16),
            pltpu.VMEM(split, bf16),
            pltpu.VMEM((N1 * CHAN, N2), f32),
            pltpu.VMEM((N1 * CHAN, N2), f32),
            pltpu.VMEM((N1 * CHAN, N2), f32),
            pltpu.VMEM((CHAN // BATCH, BATCH * N1, 2 * N2), f32),
            pltpu.VMEM((PLANE, CHAN, TOK), bf16),
            pltpu.VMEM((RING, PLANE, CHAN, TOK), bf16),
            pltpu.VMEM((GROUP, 64, D), bf16),
            pltpu.VMEM((SLAB, TOK), f32),
            pltpu.VMEM((GROUP, 64, TOK), bf16),
            pltpu.VMEM((GROUP, 64, TOK), bf16),
            dma((CTX,)), dma((CTX,)), dma((CTX,)), dma((CTX,)),
            dma((4,)), dma((4,)), dma((4,)), dma((4,)),
            dma((PLANE,)), dma((PLANE,)),
            dma((4, 2)), dma((4, 2)), dma((4, 2)), dma((4, 2)),
            dma((GROUP,)), dma((GROUP,)),
        ],
        compiler_params=pltpu.CompilerParams(
            collective_id=0, has_side_effects=True, vmem_limit_bytes=48 * 1024 * 1024
        ),
    )(
        query_gate.reshape(split),
        key_gate.reshape(split),
        value_proj.reshape(split),
        filter_taps,
        out_weight,
        *[jnp.asarray(t) for t in tables()],
    )


def solution(mesh):
    return jax.shard_map(
        per_device,
        mesh=mesh,
        in_specs=(P("ch", "ctx"), P("ch", "ctx"), P("ch", "ctx"), P("ch", None), P(None, "ch")),
        out_specs=P("ch", "ctx"),
        check_vma=False,
    )
```

```python
import jax
import jax.numpy as jnp
import ml_dtypes
import numpy as np
from jax import lax
from jax.experimental import pallas as pl
from jax.experimental.pallas import tpu as pltpu
from jax.sharding import PartitionSpec as P

SEQ = 8192
N1 = 64
N2 = 128
CTX = 4
GROUP = 8
CHAN = 16
BATCH = 4
RING = 8
PLANE = CTX * GROUP
TOK = 256
D = 4096
SLAB = D // RING
MESH = pl.DeviceIdType.MESH

bf16 = jnp.bfloat16
f32 = jnp.float32


def two_parts(table):
    high = table.astype(ml_dtypes.bfloat16)
    low = (table - high.astype(np.float64)).astype(ml_dtypes.bfloat16)
    return high, low


def tables():
    root = np.pi / (2 * SEQ)
    n1, k1, n2, k2 = np.arange(N1), np.arange(N1), np.arange(N2), np.arange(N2)
    first = np.exp(1j * (root * N2 * n1[None, :] - 2 * np.pi * k1[:, None] * n1[None, :] / N1))
    twist = np.exp(1j * (root * n2[None, :] - 2 * np.pi * k1[:, None] * n2[None, :] / SEQ))
    second = np.exp(-2j * np.pi * n2[:, None] * k2[None, :] / N2)
    high, low = two_parts(np.concatenate([first.real, first.imag], axis=0))
    stage1 = np.concatenate([high, low], axis=1)
    fwd = two_parts(np.block([[second.real, second.imag], [-second.imag, second.real]]))
    inv = two_parts(np.block([[second.real, -second.imag], [second.imag, second.real]]))
    high, low = two_parts(np.concatenate([first.real.T, first.imag.T], axis=1) / SEQ)
    last = np.concatenate([high, low], axis=1)
    twist2 = np.concatenate([twist.real, twist.imag], axis=1).astype(np.float32)
    return stage1, np.stack(fwd), np.stack(inv), last, twist2


def dot(a, b):
    return jnp.dot(a, b, preferred_element_type=f32)


def parts_of(x):
    high = x.astype(bf16)
    return high, (x - high.astype(f32)).astype(bf16)


def dot3(x, table_ref):
    high, low = parts_of(x)
    return dot(high, table_ref[0]) + (dot(low, table_ref[0]) + dot(high, table_ref[1]))


def spectrum(ref, c0, stage1, tw_re, tw_im, fwd_ref):
    rows = []
    for c in range(BATCH):
        x = ref[pl.ds(c0 + c, N1, stride=CHAN), :].astype(bf16)
        a = dot(stage1, jnp.concatenate([x, x], axis=0))
        re, im = a[:N1], a[N1:]
        rows.append(jnp.concatenate([re * tw_re - im * tw_im, re * tw_im + im * tw_re], axis=1))
    return dot3(jnp.concatenate(rows, axis=0), fwd_ref)


def layer_kernel(
    q_in, k_in, v_in, f_in, w_in, s1_in, fwd_in, inv_in, last_in, tw_in,
    out_ref,
    q_ref, k_ref, v_ref, f_ref, s1_ref, fwd_ref, inv_ref, last_ref, tw_ref,
    prod, pbuf, qbuf, sig, filt, conv, fspec, gsend, gbuf, wbuf, acc, osend, obuf,
    load_sem,
    p_send, p_recv, q_send, q_recv, w_send, w_recv, s_send, s_recv,
    g_send, g_recv, r_send, r_recv, l_send, l_recv, o_send, o_recv,
):
    ctx = lax.axis_index("ctx")
    ch = lax.axis_index("ch")
    z, j = ch // GROUP, ch % GROUP
    x, core = j // 2, j % 2
    me = ctx * GROUP + j

    def at(other_ctx, other_z, other_j):
        return (other_ctx, other_z * GROUP + other_j)

    def send(src, dst, send_sem, recv_sem, device):
        copy = pltpu.make_async_remote_copy(
            src_ref=src, dst_ref=dst, send_sem=send_sem, recv_sem=recv_sem,
            device_id=device, device_id_type=MESH,
        )
        copy.start()
        unsent.append(copy)
        unreceived.append(copy)
        return copy

    unsent, unreceived = [], []
    scattered = False

    def take_in(copies):
        for copy in copies:
            copy.wait_recv()
            unreceived[:] = [other for other in unreceived if other is not copy]

    up, down = at(ctx, (z + 1) % RING, j), at(ctx, (z + RING - 1) % RING, j)
    pairs = [
        (k_in, k_ref), (v_in, v_ref), (f_in, f_ref), (s1_in, s1_ref), (fwd_in, fwd_ref),
        (tw_in, tw_ref), (q_in, q_ref), (inv_in, inv_ref), (last_in, last_ref),
        (w_in, wbuf.at[j]),
    ]
    loads = [
        pltpu.make_async_copy(src, dst, load_sem.at[i]) for i, (src, dst) in enumerate(pairs)
    ]
    for copy in loads:
        copy.start()
    barrier = pltpu.get_barrier_semaphore()

    def greet(i, _):
        peer = (me + 1 + i) % PLANE
        pl.semaphore_signal(
            barrier, inc=1, device_id=at(peer // GROUP, z, peer % GROUP), device_id_type=MESH
        )
        return 0

    lax.fori_loop(0, PLANE - 1, greet, 0)
    pl.semaphore_signal(barrier, inc=1, device_id=up, device_id_type=MESH)
    pl.semaphore_signal(barrier, inc=1, device_id=down, device_id_type=MESH)

    loads[0].wait()
    loads[1].wait()
    prod[...] = (k_ref[...].astype(f32) * v_ref[...].astype(f32)).astype(bf16)
    pl.semaphore_wait(barrier, PLANE + 1)

    def spread(src, dst, send_sem, recv_sem):
        peers = [(ctx + i) % CTX for i in range(1, CTX)]
        return [
            send(src.at[peer], dst.at[ctx], send_sem.at[i], recv_sem.at[i], at(peer, z, j))
            for i, peer in enumerate(peers)
        ]

    p_waits = spread(prod, pbuf, p_send, p_recv)
    pbuf[ctx] = prod[ctx]

    xr, xl = (x + 1) % 4, (x + 3) % 4
    right, left = at(ctx, z, xr * 2 + core), at(ctx, z, xl * 2 + core)
    sibling = at(ctx, z, x * 2 + 1 - core)
    j_right, j_left, j_far = xr * 2 + core, xl * 2 + core, ((x + 2) % 4) * 2 + core
    w_waits = [
        send(w_in, wbuf.at[j], w_send.at[0], w_recv.at[0], right),
        send(w_in, wbuf.at[j], w_send.at[1], w_recv.at[1], left),
    ]
    s_waits = [send(w_in, wbuf.at[j], s_send.at[0], s_recv.at[0], sibling)]
    q_waits = spread(q_in, qbuf, q_send, q_recv)

    for copy in loads[2:]:
        copy.wait()
    qbuf[ctx] = q_ref[ctx]

    own = pl.ds(pl.multiple_of(ctx * CHAN, CHAN), CHAN)
    for n in range(N1):
        filt[n * CHAN : (n + 1) * CHAN, :] = f_ref[own, n * N2 : (n + 1) * N2].astype(f32)
    stage1 = s1_ref[...]
    tw_re, tw_im = tw_ref[:, :N2], tw_ref[:, N2:]

    def filter_step(i, _):
        fspec[i] = spectrum(filt, i * BATCH, stage1, tw_re, tw_im, fwd_ref)
        return 0

    lax.fori_loop(0, CHAN // BATCH, filter_step, 0)

    take_in(p_waits)
    for n in range(N1):
        col = (n % 16) * N2
        sig[n * CHAN : (n + 1) * CHAN, :] = pbuf[n // 16, :, col : col + N2].astype(f32)

    def conv_step(i, _):
        c0 = i * BATCH
        fs = fspec[i]
        ss = spectrum(sig, c0, stage1, tw_re, tw_im, fwd_ref)
        fr, fi, sr, si = fs[:, :N2], fs[:, N2:], ss[:, :N2], ss[:, N2:]
        back = dot3(jnp.concatenate([fr * sr - fi * si, fr * si + fi * sr], axis=1), inv_ref)
        last = last_ref[...]
        for c in range(BATCH):
            re = back[c * N1 : (c + 1) * N1, :N2]
            im = back[c * N1 : (c + 1) * N1, N2:]
            u = jnp.concatenate([re * tw_re + im * tw_im, im * tw_re - re * tw_im], axis=0)
            high, low = parts_of(u)
            y = dot(last, jnp.concatenate([high, high], axis=0)) + dot(last[:, :N2], low)
            conv[pl.ds(c0 + c, N1, stride=CHAN), :] = y
        return 0

    lax.fori_loop(0, CHAN // BATCH, conv_step, 0)

    take_in(q_waits)
    for n in range(N1):
        col = (n % 16) * N2
        gate = qbuf[n // 16, :, col : col + N2].astype(f32)
        gsend[n // 2, :, (n % 2) * N2 : (n % 2 + 1) * N2] = (
            gate * conv[n * CHAN : (n + 1) * CHAN, :]
        ).astype(bf16)

    slot = j * CTX + ctx

    def tile_copy(i):
        peer = (me + i) % PLANE
        return pltpu.make_async_remote_copy(
            src_ref=gsend.at[peer], dst_ref=gbuf.at[z, slot], send_sem=g_send.at[i],
            recv_sem=g_recv.at[slot], device_id=at(peer // GROUP, z, peer % GROUP),
            device_id_type=MESH,
        )

    def scatter(i, _):
        tile_copy(i).start()
        return 0

    lax.fori_loop(1, PLANE, scatter, 0)
    scattered = True
    gbuf[z, slot] = gsend[me]

    def arrived(i, _):
        @pl.when(i != slot)
        def _():
            pltpu.make_async_remote_copy(
                src_ref=gsend.at[0], dst_ref=gbuf.at[z, i], send_sem=g_send.at[0],
                recv_sem=g_recv.at[i], device_id=up, device_id_type=MESH,
            ).wait_recv()

        return 0

    half = PLANE // 2

    def pass_on(step, h):
        rows = pl.ds(h * half, half)
        up_slab, down_slab = (z + RING - step) % RING, (z + step) % RING
        ups = downs = None
        if step < 3 or h == 0:
            part = gbuf.at[up_slab, rows]
            ups = send(part, part, r_send.at[step, h], r_recv.at[step, h], up)
        if step < 3 or h == 1:
            part = gbuf.at[down_slab, rows]
            downs = send(part, part, l_send.at[step, h], l_recv.at[step, h], down)
        return ups, downs

    hops = {}
    for h in range(2):
        lax.fori_loop(h * half, (h + 1) * half, arrived, 0)
        hops[0, h] = pass_on(0, h)

    take_in([w_waits[0]])
    part = wbuf.at[j_left, pl.ds(0, 32)]
    w_waits.append(send(part, part, w_send.at[2], w_recv.at[2], right))
    part = wbuf.at[j_left]
    s_waits.append(send(part, part, s_send.at[1], s_recv.at[1], sibling))
    take_in([w_waits[1]])
    part = wbuf.at[j_right, pl.ds(32, 32)]
    w_waits.append(send(part, part, w_send.at[3], w_recv.at[3], left))
    part = wbuf.at[j_right]
    s_waits.append(send(part, part, s_send.at[2], s_recv.at[2], sibling))

    def take(step):
        for h in range(2):
            ups, downs = hops[step, h]
            take_in([copy for copy in (ups, downs) if copy is not None])
            if step < 3:
                hops[step + 1, h] = pass_on(step + 1, h)

    def project(offset, first=False):
        slab = (z + offset) % RING
        cols = pl.ds(pl.multiple_of(slab * SLAB, SLAB), SLAB)
        weight = wbuf[:, :, cols].reshape(SLAB, SLAB)
        term = dot(weight, gbuf[slab].reshape(SLAB, TOK))
        acc[...] = term if first else acc[...] + term

    take(0)
    take_in(w_waits[2:])
    part = wbuf.at[j_far]
    s_waits.append(send(part, part, s_send.at[3], s_recv.at[3], sibling))
    take(1)
    take_in(s_waits)
    project(0, first=True)
    project(1)
    project(RING - 1)
    take(2)
    project(2)
    project(RING - 2)
    project(3)
    project(RING - 3)
    take(3)
    project(4)

    osend[...] = acc[...].reshape(GROUP, 64, TOK).astype(bf16)
    o_waits = []
    for i in range(1, GROUP):
        peer = (j + i) % GROUP
        o_waits.append(
            send(osend.at[peer], obuf.at[j], o_send.at[i], o_recv.at[i], at(ctx, z, peer))
        )
    obuf[j] = osend[j]
    take_in(o_waits)
    for i in range(GROUP):
        out_ref[:, i * TOK : (i + 1) * TOK] = obuf[i]

    for copy in unsent:
        copy.wait_send()

    def sent(i, _):
        tile_copy(i).wait_send()
        return 0

    lax.fori_loop(1, PLANE, sent, 0)


def per_device(query_gate, key_gate, value_proj, filter_taps, out_weight):
    tokens = SEQ // CTX
    split = (CTX, CHAN, tokens)
    dma = pltpu.SemaphoreType.DMA
    consts = [jnp.asarray(t) for t in tables()]
    return pl.pallas_call(
        layer_kernel,
        out_shape=jax.ShapeDtypeStruct((CTX * CHAN, tokens), bf16),
        in_specs=[pl.BlockSpec(memory_space=pl.ANY)] * 10,
        out_specs=pl.BlockSpec(memory_space=pltpu.VMEM),
        scratch_shapes=[
            pltpu.VMEM(split, bf16),
            pltpu.VMEM(split, bf16),
            pltpu.VMEM(split, bf16),
            pltpu.VMEM((CTX * CHAN, SEQ), bf16),
            *[pltpu.VMEM(t.shape, t.dtype) for t in consts],
            pltpu.VMEM(split, bf16),
            pltpu.VMEM(split, bf16),
            pltpu.VMEM(split, bf16),
            pltpu.VMEM((N1 * CHAN, N2), f32),
            pltpu.VMEM((N1 * CHAN, N2), f32),
            pltpu.VMEM((N1 * CHAN, N2), f32),
            pltpu.VMEM((CHAN // BATCH, BATCH * N1, 2 * N2), f32),
            pltpu.VMEM((PLANE, CHAN, TOK), bf16),
            pltpu.VMEM((RING, PLANE, CHAN, TOK), bf16),
            pltpu.VMEM((GROUP, 64, D), bf16),
            pltpu.VMEM((SLAB, TOK), f32),
            pltpu.VMEM((GROUP, 64, TOK), bf16),
            pltpu.VMEM((GROUP, 64, TOK), bf16),
            dma((10,)),
            dma((CTX - 1,)), dma((CTX - 1,)), dma((CTX - 1,)), dma((CTX - 1,)),
            dma((4,)), dma((4,)), dma((4,)), dma((4,)),
            dma((PLANE,)), dma((PLANE,)),
            dma((4, 2)), dma((4, 2)), dma((4, 2)), dma((4, 2)),
            dma((GROUP,)), dma((GROUP,)),
        ],
        compiler_params=pltpu.CompilerParams(
            collective_id=0, has_side_effects=True, vmem_limit_bytes=56 * 1024 * 1024
        ),
    )(
        query_gate.reshape(split),
        key_gate.reshape(split),
        value_proj.reshape(split),
        filter_taps,
        out_weight.T,
        *consts,
    )


def solution(mesh):
    return jax.shard_map(
        per_device,
        mesh=mesh,
        in_specs=(P("ch", "ctx"), P("ch", "ctx"), P("ch", "ctx"), P("ch", None), P(None, "ch")),
        out_specs=P("ch", "ctx"),
        check_vma=False,
    )
```

```python
import jax
import jax.numpy as jnp
import ml_dtypes
import numpy as np
from jax import lax
from jax.experimental import pallas as pl
from jax.experimental.pallas import tpu as pltpu
from jax.sharding import PartitionSpec as P

SEQ = 8192
N1 = 64
N2 = 128
CTX = 4
GROUP = 8
CHAN = 16
BATCH = 4
RING = 8
PLANE = CTX * GROUP
TOK = 256
D = 4096
SLAB = D // RING
PART = PLANE // 4
NEAR = (0, 1, 3, 2)
MESH = pl.DeviceIdType.MESH

bf16 = jnp.bfloat16
f32 = jnp.float32


def two_parts(table):
    high = table.astype(ml_dtypes.bfloat16)
    low = (table - high.astype(np.float64)).astype(ml_dtypes.bfloat16)
    return high, low


def tables():
    root = np.pi / (2 * SEQ)
    n1, k1, n2, k2 = np.arange(N1), np.arange(N1), np.arange(N2), np.arange(N2)
    first = np.exp(1j * (root * N2 * n1[None, :] - 2 * np.pi * k1[:, None] * n1[None, :] / N1))
    twist = np.exp(1j * (root * n2[None, :] - 2 * np.pi * k1[:, None] * n2[None, :] / SEQ))
    second = np.exp(-2j * np.pi * n2[:, None] * k2[None, :] / N2)
    high, low = two_parts(np.concatenate([first.real, first.imag], axis=0))
    stage1 = np.concatenate([high, low], axis=1)
    fwd = two_parts(np.block([[second.real, second.imag], [-second.imag, second.real]]))
    inv = two_parts(np.block([[second.real, -second.imag], [second.imag, second.real]]))
    high, low = two_parts(np.concatenate([first.real.T, first.imag.T], axis=1) / SEQ)
    last = np.concatenate([high, low], axis=1)
    twist2 = two_parts(np.concatenate([twist.real, twist.imag], axis=1))
    stage1 = np.concatenate([stage1, np.zeros_like(stage1)], axis=1)
    return np.concatenate([*fwd, *inv, last, stage1, *twist2], axis=0)


FWD, INV, LAST, STAGE1, TWIST, END = np.cumsum([0, 4 * N2, 4 * N2, N1, 2 * N1, 2 * N1]).tolist()


def dot(a, b):
    return jnp.dot(a, b, preferred_element_type=f32)


def parts_of(x):
    high = x.astype(bf16)
    return high, (x - high.astype(f32)).astype(bf16)


def dot3(x, table_ref):
    high, low = parts_of(x)
    first, second = table_ref[: 2 * N2], table_ref[2 * N2 :]
    return dot(high, first) + (dot(low, first) + dot(high, second))


def spectrum(ref, c0, stage1, tw_re, tw_im, fwd_ref):
    rows = []
    for c in range(BATCH):
        x = ref[pl.ds(c0 + c, N1, stride=CHAN), :].astype(bf16)
        a = dot(stage1, jnp.concatenate([x, x], axis=0))
        re, im = a[:N1], a[N1:]
        rows.append(jnp.concatenate([re * tw_re - im * tw_im, re * tw_im + im * tw_re], axis=1))
    return dot3(jnp.concatenate(rows, axis=0), fwd_ref)


def layer_kernel(
    q_in, k_in, v_in, f_in, w_in, table_in,
    out_ref,
    q_ref, k_ref, v_ref, f_ref, table, tw_ref,
    prod, pbuf, qbuf, sig, filt, conv, fspec, gsend, gbuf, wbuf, acc, osend, obuf,
    load_sem,
    p_send, p_recv, q_send, q_recv, w_send, w_recv, s_send, s_recv,
    g_send, g_recv, r_send, r_recv, l_send, l_recv, o_send, o_recv,
):
    ctx = lax.axis_index("ctx")
    ch = lax.axis_index("ch")
    z, j = ch // GROUP, ch % GROUP
    x, core = j // 2, j % 2
    me = ctx * GROUP + j

    def at(other_ctx, other_z, other_j):
        return (other_ctx, other_z * GROUP + other_j)

    def send(src, dst, send_sem, recv_sem, device):
        copy = pltpu.make_async_remote_copy(
            src_ref=src, dst_ref=dst, send_sem=send_sem, recv_sem=recv_sem,
            device_id=device, device_id_type=MESH,
        )
        copy.start()
        unsent.append(copy)
        unreceived.append(copy)
        return copy

    unsent, unreceived = [], []
    scattered = False

    def take_in(copies):
        for copy in copies:
            copy.wait_recv()
            unreceived[:] = [other for other in unreceived if other is not copy]

    up, down = at(ctx, (z + 1) % RING, j), at(ctx, (z + RING - 1) % RING, j)
    pairs = [
        (k_in, k_ref), (v_in, v_ref), (f_in, f_ref), (table_in, table), (q_in, q_ref),
        (w_in, wbuf.at[j]),
    ]
    loads = [
        pltpu.make_async_copy(src, dst, load_sem.at[i]) for i, (src, dst) in enumerate(pairs)
    ]
    for copy in loads:
        copy.start()
    barrier = pltpu.get_barrier_semaphore()

    def greet(i, _):
        peer = (me + 1 + i) % PLANE
        pl.semaphore_signal(
            barrier, inc=1, device_id=at(peer // GROUP, z, peer % GROUP), device_id_type=MESH
        )
        return 0

    lax.fori_loop(0, PLANE - 1, greet, 0)
    pl.semaphore_signal(barrier, inc=1, device_id=up, device_id_type=MESH)
    pl.semaphore_signal(barrier, inc=1, device_id=down, device_id_type=MESH)

    loads[0].wait()
    loads[1].wait()
    prod[...] = (k_ref[...].astype(f32) * v_ref[...].astype(f32)).astype(bf16)
    pl.semaphore_wait(barrier, PLANE + 1)

    def spread(src, dst, send_sem, recv_sem):
        peers = [(ctx + i) % CTX for i in range(1, CTX)]
        return [
            send(src.at[peer], dst.at[ctx], send_sem.at[i], recv_sem.at[i], at(peer, z, j))
            for i, peer in enumerate(peers)
        ]

    p_waits = spread(prod, pbuf, p_send, p_recv)
    pbuf[ctx] = prod[ctx]

    xr, xl = (x + 1) % 4, (x + 3) % 4
    right, left = at(ctx, z, xr * 2 + core), at(ctx, z, xl * 2 + core)
    sibling = at(ctx, z, x * 2 + 1 - core)
    j_right, j_left, j_far = xr * 2 + core, xl * 2 + core, ((x + 2) % 4) * 2 + core
    w_waits = [
        send(w_in, wbuf.at[j], w_send.at[0], w_recv.at[0], right),
        send(w_in, wbuf.at[j], w_send.at[1], w_recv.at[1], left),
    ]
    s_waits = [send(w_in, wbuf.at[j], s_send.at[0], s_recv.at[0], sibling)]
    q_waits = spread(q_in, qbuf, q_send, q_recv)

    for copy in loads[2:]:
        copy.wait()
    qbuf[ctx] = q_ref[ctx]

    own = pl.ds(pl.multiple_of(ctx * CHAN, CHAN), CHAN)
    for n in range(N1):
        filt[n * CHAN : (n + 1) * CHAN, :] = f_ref[own, n * N2 : (n + 1) * N2].astype(f32)
    fwd_ref, inv_ref = table.at[FWD:INV], table.at[INV:LAST]
    stage1 = table[STAGE1:TWIST, : 2 * N1]
    twist = table[TWIST:END, :].astype(f32)
    tw_ref[...] = twist[:N1] + twist[N1:]
    tw_re, tw_im = tw_ref[:, :N2], tw_ref[:, N2:]

    def filter_step(i, _):
        fspec[i] = spectrum(filt, i * BATCH, stage1, tw_re, tw_im, fwd_ref)
        return 0

    lax.fori_loop(0, CHAN // BATCH, filter_step, 0)

    take_in(p_waits)
    for n in range(N1):
        col = (n % 16) * N2
        sig[n * CHAN : (n + 1) * CHAN, :] = pbuf[n // 16, :, col : col + N2].astype(f32)

    def conv_step(i, _):
        c0 = i * BATCH
        fs = fspec[i]
        ss = spectrum(sig, c0, stage1, tw_re, tw_im, fwd_ref)
        fr, fi, sr, si = fs[:, :N2], fs[:, N2:], ss[:, :N2], ss[:, N2:]
        back = dot3(jnp.concatenate([fr * sr - fi * si, fr * si + fi * sr], axis=1), inv_ref)
        last = table[LAST:STAGE1, :]
        for c in range(BATCH):
            re = back[c * N1 : (c + 1) * N1, :N2]
            im = back[c * N1 : (c + 1) * N1, N2:]
            u = jnp.concatenate([re * tw_re + im * tw_im, im * tw_re - re * tw_im], axis=0)
            high, low = parts_of(u)
            y = dot(last, jnp.concatenate([high, high], axis=0)) + dot(last[:, :N2], low)
            conv[pl.ds(c0 + c, N1, stride=CHAN), :] = y
        return 0

    lax.fori_loop(0, CHAN // BATCH, conv_step, 0)

    take_in(q_waits)
    slot = j * CTX + ctx

    def tile_copy(peer_ctx, peer_j):
        peer = peer_ctx * GROUP + peer_j
        return pltpu.make_async_remote_copy(
            src_ref=gsend.at[peer], dst_ref=gbuf.at[z, slot], send_sem=g_send.at[peer],
            recv_sem=g_recv.at[slot], device_id=at(peer_ctx, z, peer_j), device_id_type=MESH,
        )

    def gated_tile(peer_ctx, peer_j):
        halves = []
        for n in range(2):
            rows = pl.ds(pl.multiple_of((peer_ctx * 16 + peer_j * 2 + n) * CHAN, CHAN), CHAN)
            cols = pl.ds(pl.multiple_of(peer_j * TOK + n * N2, N2), N2)
            halves.append((qbuf[peer_ctx, :, cols].astype(f32) * conv[rows, :]).astype(bf16))
        return jnp.concatenate(halves, axis=1)

    def scatter(i, dx):
        peer_ctx, peer_j = (ctx + i // 2) % CTX, (x + dx) % 4 * 2 + (core + i) % 2
        gsend[peer_ctx * GROUP + peer_j] = gated_tile(peer_ctx, peer_j)
        tile_copy(peer_ctx, peer_j).start()
        return dx

    for dx in NEAR:
        lax.fori_loop(0 if dx else 1, PART, scatter, dx)
    gbuf[z, slot] = gated_tile(ctx, j)
    scattered = True

    def arrived(i, _):
        @pl.when(i != slot)
        def _():
            pltpu.make_async_remote_copy(
                src_ref=gsend.at[0], dst_ref=gbuf.at[z, i], send_sem=g_send.at[0],
                recv_sem=g_recv.at[i], device_id=up, device_id_type=MESH,
            ).wait_recv()

        return 0

    def pass_on(step, h):
        rows = pl.ds((x + 4 - NEAR[h]) % 4 * PART, PART)
        up_slab, down_slab = (z + RING - step) % RING, (z + step) % RING
        ups = downs = None
        if step < 3 or h < 2:
            part = gbuf.at[up_slab, rows]
            ups = send(part, part, r_send.at[step, h], r_recv.at[step, h], up)
        if step < 3 or h >= 2:
            part = gbuf.at[down_slab, rows]
            downs = send(part, part, l_send.at[step, h], l_recv.at[step, h], down)
        return ups, downs

    hops = {}
    for h in range(4):
        first = (x + 4 - NEAR[h]) % 4 * PART
        lax.fori_loop(first, first + PART, arrived, 0)
        hops[0, h] = pass_on(0, h)

    take_in([w_waits[0]])
    part = wbuf.at[j_left, pl.ds(0, 32)]
    w_waits.append(send(part, part, w_send.at[2], w_recv.at[2], right))
    part = wbuf.at[j_left]
    s_waits.append(send(part, part, s_send.at[1], s_recv.at[1], sibling))
    take_in([w_waits[1]])
    part = wbuf.at[j_right, pl.ds(32, 32)]
    w_waits.append(send(part, part, w_send.at[3], w_recv.at[3], left))
    part = wbuf.at[j_right]
    s_waits.append(send(part, part, s_send.at[2], s_recv.at[2], sibling))

    def take(step):
        for h in range(4):
            ups, downs = hops[step, h]
            take_in([copy for copy in (ups, downs) if copy is not None])
            if step < 3:
                hops[step + 1, h] = pass_on(step + 1, h)

    def project(offset, first=False):
        slab = (z + offset) % RING
        cols = pl.ds(pl.multiple_of(slab * SLAB, SLAB), SLAB)
        weight = wbuf[:, :, cols].reshape(SLAB, SLAB)
        term = dot(weight, gbuf[slab].reshape(SLAB, TOK))
        acc[...] = term if first else acc[...] + term

    take(0)
    take_in(w_waits[2:])
    part = wbuf.at[j_far]
    s_waits.append(send(part, part, s_send.at[3], s_recv.at[3], sibling))
    take(1)
    take_in(s_waits)
    project(0, first=True)
    project(1)
    project(RING - 1)
    take(2)
    project(2)
    project(RING - 2)
    project(3)
    project(RING - 3)
    take(3)
    project(4)

    o_waits = []
    for i in range(1, GROUP):
        peer = (j + i) % GROUP
        rows = pl.ds(pl.multiple_of(peer * 64, 64), 64)
        osend[peer] = acc[rows, :].astype(bf16)
        o_waits.append(
            send(osend.at[peer], obuf.at[j], o_send.at[i], o_recv.at[i], at(ctx, z, peer))
        )
    obuf[j] = acc[pl.ds(pl.multiple_of(j * 64, 64), 64), :].astype(bf16)
    take_in(o_waits)
    for i in range(GROUP):
        out_ref[:, i * TOK : (i + 1) * TOK] = obuf[i]

    for copy in unsent:
        copy.wait_send()

    def sent(i, _):
        tile_copy((ctx + i // GROUP) % CTX, (j + i) % GROUP).wait_send()
        return 0

    lax.fori_loop(1, PLANE, sent, 0)


def per_device(query_gate, key_gate, value_proj, filter_taps, out_weight):
    tokens = SEQ // CTX
    split = (CTX, CHAN, tokens)
    dma = pltpu.SemaphoreType.DMA
    return pl.pallas_call(
        layer_kernel,
        out_shape=jax.ShapeDtypeStruct((CTX * CHAN, tokens), bf16),
        in_specs=[pl.BlockSpec(memory_space=pl.ANY)] * 6,
        out_specs=pl.BlockSpec(memory_space=pltpu.VMEM),
        scratch_shapes=[
            pltpu.VMEM(split, bf16),
            pltpu.VMEM(split, bf16),
            pltpu.VMEM(split, bf16),
            pltpu.VMEM((CTX * CHAN, SEQ), bf16),
            pltpu.VMEM((END, 2 * N2), bf16),
            pltpu.VMEM((N1, 2 * N2), f32),
            pltpu.VMEM(split, bf16),
            pltpu.VMEM(split, bf16),
            pltpu.VMEM(split, bf16),
            pltpu.VMEM((N1 * CHAN, N2), f32),
            pltpu.VMEM((N1 * CHAN, N2), f32),
            pltpu.VMEM((N1 * CHAN, N2), f32),
            pltpu.VMEM((CHAN // BATCH, BATCH * N1, 2 * N2), f32),
            pltpu.VMEM((PLANE, CHAN, TOK), bf16),
            pltpu.VMEM((RING, PLANE, CHAN, TOK), bf16),
            pltpu.VMEM((GROUP, 64, D), bf16),
            pltpu.VMEM((SLAB, TOK), f32),
            pltpu.VMEM((GROUP, 64, TOK), bf16),
            pltpu.VMEM((GROUP, 64, TOK), bf16),
            dma((6,)),
            dma((CTX - 1,)), dma((CTX - 1,)), dma((CTX - 1,)), dma((CTX - 1,)),
            dma((4,)), dma((4,)), dma((4,)), dma((4,)),
            dma((PLANE,)), dma((PLANE,)),
            dma((4, 4)), dma((4, 4)), dma((4, 4)), dma((4, 4)),
            dma((GROUP,)), dma((GROUP,)),
        ],
        compiler_params=pltpu.CompilerParams(
            collective_id=0, has_side_effects=True, vmem_limit_bytes=54720 * 1024
        ),
    )(
        query_gate.reshape(split),
        key_gate.reshape(split),
        value_proj.reshape(split),
        filter_taps,
        out_weight.T,
        jnp.asarray(tables()),
    )


def solution(mesh):
    return jax.shard_map(
        per_device,
        mesh=mesh,
        in_specs=(P("ch", "ctx"), P("ch", "ctx"), P("ch", "ctx"), P("ch", None), P(None, "ch")),
        out_specs=P("ch", "ctx"),
        check_vma=False,
    )
```

```python
import jax
import jax.numpy as jnp
import ml_dtypes
import numpy as np
from jax import lax
from jax.experimental import pallas as pl
from jax.experimental.pallas import tpu as pltpu
from jax.sharding import PartitionSpec as P

SEQ = 8192
N1 = 64
N2 = 128
CTX = 4
GROUP = 8
CHAN = 16
BATCH = 8
RING = 8
PLANE = CTX * GROUP
TOK = 256
D = 4096
SLAB = D // RING
PART = PLANE // 4
MESH = pl.DeviceIdType.MESH

bf16 = jnp.bfloat16
f32 = jnp.float32


def two_parts(table):
    high = table.astype(ml_dtypes.bfloat16)
    low = (table - high.astype(np.float64)).astype(ml_dtypes.bfloat16)
    return high, low


def tables():
    root = np.pi / (2 * SEQ)
    n1, k1, n2, k2 = np.arange(N1), np.arange(N1), np.arange(N2), np.arange(N2)
    first = np.exp(1j * (root * N2 * n1[None, :] - 2 * np.pi * k1[:, None] * n1[None, :] / N1))
    twist = np.exp(1j * (root * n2[None, :] - 2 * np.pi * k1[:, None] * n2[None, :] / SEQ))
    second = np.exp(-2j * np.pi * n2[:, None] * k2[None, :] / N2)
    high, low = two_parts(np.concatenate([first.real, first.imag], axis=0))
    stage1 = np.concatenate([high, low], axis=1)
    fwd = two_parts(np.block([[second.real, second.imag], [-second.imag, second.real]]))
    inv = two_parts(np.block([[second.real, -second.imag], [second.imag, second.real]]))
    high, low = two_parts(np.concatenate([first.real.T, first.imag.T], axis=1) / SEQ)
    last = np.concatenate([high, low], axis=1)
    twist2 = two_parts(np.concatenate([twist.real, twist.imag], axis=1))
    stage1 = np.concatenate([stage1, np.zeros_like(stage1)], axis=1)
    return np.concatenate([*fwd, *inv, last, stage1, *twist2], axis=0)


FWD, INV, LAST, STAGE1, TWIST, END = np.cumsum([0, 4 * N2, 4 * N2, N1, 2 * N1, 2 * N1]).tolist()


def dot(a, b):
    return jnp.dot(a, b, preferred_element_type=f32)


def parts_of(x):
    high = x.astype(bf16)
    return high, (x - high.astype(f32)).astype(bf16)


def dot3(x, table_ref):
    high, low = parts_of(x)
    first, second = table_ref[: 2 * N2], table_ref[2 * N2 :]
    return dot(high, first) + (dot(low, first) + dot(high, second))


def spectrum(ref, c0, stage1, tw_re, tw_im, fwd_ref):
    rows = []
    for c in range(BATCH):
        x = ref[pl.ds(c0 + c, N1, stride=CHAN), :].astype(bf16)
        a = dot(stage1, jnp.concatenate([x, x], axis=0))
        re, im = a[:N1], a[N1:]
        rows.append(jnp.concatenate([re * tw_re - im * tw_im, re * tw_im + im * tw_re], axis=1))
    return dot3(jnp.concatenate(rows, axis=0), fwd_ref)


def layer_kernel(
    q_in, k_in, v_in, f_in, w_in, table_in,
    out_ref,
    q_ref, k_ref, v_ref, f_ref, table, tw_ref,
    prod, pbuf, qbuf, sig, filt, conv, fspec, gsend, gbuf, wbuf, acc, osend, obuf,
    load_sem,
    p_send, p_recv, q_send, q_recv, w_send, w_recv, s_send, s_recv,
    g_send, g_recv, r_send, r_recv, l_send, l_recv, o_send, o_recv,
):
    ctx = lax.axis_index("ctx")
    ch = lax.axis_index("ch")
    z, j = ch // GROUP, ch % GROUP
    x, core = j // 2, j % 2
    me = ctx * GROUP + j

    def at(other_ctx, other_z, other_j):
        return (other_ctx, other_z * GROUP + other_j)

    def send(src, dst, send_sem, recv_sem, device):
        copy = pltpu.make_async_remote_copy(
            src_ref=src, dst_ref=dst, send_sem=send_sem, recv_sem=recv_sem,
            device_id=device, device_id_type=MESH,
        )
        copy.start()
        unsent.append(copy)
        unreceived.append(copy)
        return copy

    unsent, unreceived = [], []
    scattered = False

    def take_in(copies):
        for copy in copies:
            copy.wait_recv()
            unreceived[:] = [other for other in unreceived if other is not copy]

    up, down = at(ctx, (z + 1) % RING, j), at(ctx, (z + RING - 1) % RING, j)
    pairs = [
        (k_in, k_ref), (v_in, v_ref), (f_in, f_ref), (table_in, table), (q_in, q_ref),
        (w_in, wbuf.at[j]),
    ]
    loads = [
        pltpu.make_async_copy(src, dst, load_sem.at[i]) for i, (src, dst) in enumerate(pairs)
    ]
    for copy in loads:
        copy.start()
    barrier = pltpu.get_barrier_semaphore()

    def greet(i, _):
        peer = (me + 1 + i) % PLANE
        pl.semaphore_signal(
            barrier, inc=1, device_id=at(peer // GROUP, z, peer % GROUP), device_id_type=MESH
        )
        return 0

    lax.fori_loop(0, PLANE - 1, greet, 0)
    pl.semaphore_signal(barrier, inc=1, device_id=up, device_id_type=MESH)
    pl.semaphore_signal(barrier, inc=1, device_id=down, device_id_type=MESH)

    loads[0].wait()
    loads[1].wait()
    prod[...] = (k_ref[...].astype(f32) * v_ref[...].astype(f32)).astype(bf16)
    pl.semaphore_wait(barrier, PLANE + 1)

    def spread(src, dst, send_sem, recv_sem):
        peers = [(ctx + i) % CTX for i in range(1, CTX)]
        return [
            send(src.at[peer], dst.at[ctx], send_sem.at[i], recv_sem.at[i], at(peer, z, j))
            for i, peer in enumerate(peers)
        ]

    p_waits = spread(prod, pbuf, p_send, p_recv)
    pbuf[ctx] = prod[ctx]

    xr, xl = (x + 1) % 4, (x + 3) % 4
    right, left = at(ctx, z, xr * 2 + core), at(ctx, z, xl * 2 + core)
    sibling = at(ctx, z, x * 2 + 1 - core)
    j_right, j_left, j_far = xr * 2 + core, xl * 2 + core, ((x + 2) % 4) * 2 + core
    low, high = pl.ds(0, 32), pl.ds(32, 32)

    def pass_weights(src, dst, i, device):
        return send(src, dst, w_send.at[i], w_recv.at[i], device)

    s_waits = []

    def to_sibling(src, dst):
        i = len(s_waits)
        s_waits.append(send(src, dst, s_send.at[i], s_recv.at[i], sibling))

    w_waits = [
        pass_weights(w_in.at[low], wbuf.at[j, low], 0, right),
        pass_weights(w_in.at[high], wbuf.at[j, high], 1, left),
    ]
    to_sibling(w_in, wbuf.at[j])
    q_waits = spread(q_in, qbuf, q_send, q_recv)

    for copy in loads[2:]:
        copy.wait()
    qbuf[ctx] = q_ref[ctx]

    own = pl.ds(pl.multiple_of(ctx * CHAN, CHAN), CHAN)

    def widen_filter(i, _):
        for k in range(CTX):
            n = k * 16 + i
            rows = pl.ds(pl.multiple_of(n * CHAN, CHAN), CHAN)
            filt[rows, :] = f_ref[own, pl.ds(pl.multiple_of(n * N2, N2), N2)].astype(f32)
        return 0

    lax.fori_loop(0, 16, widen_filter, 0)
    fwd_ref, inv_ref = table.at[FWD:INV], table.at[INV:LAST]
    stage1 = table[STAGE1:TWIST, : 2 * N1]
    twist = table[TWIST:END, :].astype(f32)
    tw_ref[...] = twist[:N1] + twist[N1:]
    tw_re, tw_im = tw_ref[:, :N2], tw_ref[:, N2:]

    def filter_step(i, _):
        fspec[i] = spectrum(filt, i * BATCH, stage1, tw_re, tw_im, fwd_ref)
        return 0

    lax.fori_loop(0, CHAN // BATCH, filter_step, 0)

    take_in(p_waits)

    def widen_signal(i, _):
        for k in range(CTX):
            rows = pl.ds(pl.multiple_of((k * 16 + i) * CHAN, CHAN), CHAN)
            sig[rows, :] = pbuf[k, :, pl.ds(pl.multiple_of(i * N2, N2), N2)].astype(f32)
        return 0

    lax.fori_loop(0, 16, widen_signal, 0)

    def conv_step(i, _):
        c0 = i * BATCH
        fs = fspec[i]
        ss = spectrum(sig, c0, stage1, tw_re, tw_im, fwd_ref)
        fr, fi, sr, si = fs[:, :N2], fs[:, N2:], ss[:, :N2], ss[:, N2:]
        back = dot3(jnp.concatenate([fr * sr - fi * si, fr * si + fi * sr], axis=1), inv_ref)
        last = table[LAST:STAGE1, :]
        for c in range(BATCH):
            re = back[c * N1 : (c + 1) * N1, :N2]
            im = back[c * N1 : (c + 1) * N1, N2:]
            u = jnp.concatenate([re * tw_re + im * tw_im, im * tw_re - re * tw_im], axis=0)
            high, low = parts_of(u)
            y = dot(last, jnp.concatenate([high, high], axis=0)) + dot(last[:, :N2], low)
            conv[pl.ds(c0 + c, N1, stride=CHAN), :] = y
        return 0

    lax.fori_loop(0, CHAN // BATCH, conv_step, 0)

    take_in(q_waits)
    slot = j * CTX + ctx

    def tile_copy(peer_ctx, peer_j):
        peer = peer_ctx * GROUP + peer_j
        return pltpu.make_async_remote_copy(
            src_ref=gsend.at[peer], dst_ref=gbuf.at[z, slot], send_sem=g_send.at[peer],
            recv_sem=g_recv.at[slot], device_id=at(peer_ctx, z, peer_j), device_id_type=MESH,
        )

    def gated_tile(peer_ctx, peer_j):
        halves = []
        for n in range(2):
            rows = pl.ds(pl.multiple_of((peer_ctx * 16 + peer_j * 2 + n) * CHAN, CHAN), CHAN)
            cols = pl.ds(pl.multiple_of(peer_j * TOK + n * N2, N2), N2)
            halves.append((qbuf[peer_ctx, :, cols].astype(f32) * conv[rows, :]).astype(bf16))
        return jnp.concatenate(halves, axis=1)

    def scatter(i, dx):
        peer_ctx, peer_j = (ctx + i // 2) % CTX, (x + 4 + dx) % 4 * 2 + (core + i) % 2
        gsend[peer_ctx * GROUP + peer_j] = gated_tile(peer_ctx, peer_j)
        tile_copy(peer_ctx, peer_j).start()
        return dx

    mate = 1 - 2 * (x % 2)
    lax.fori_loop(1, PART, scatter, 0)
    for dx in (mate, 4 - mate, 2):
        lax.fori_loop(0, PART, scatter, dx)
    gbuf[z, slot] = gated_tile(ctx, j)
    scattered = True

    def arrived(i, _):
        @pl.when(i != slot)
        def _():
            pltpu.make_async_remote_copy(
                src_ref=gsend.at[0], dst_ref=gbuf.at[z, i], send_sem=g_send.at[0],
                recv_sem=g_recv.at[i], device_id=up, device_id_type=MESH,
            ).wait_recv()

        return 0

    near = x // 2 * 2 * PART
    firsts = (x * PART, (x + mate) * PART, 2 * PART - near)

    def pass_on(step, h):
        rows = pl.ds(near if h == 3 else firsts[h], PART if h < 2 else 2 * PART)
        up_slab, down_slab = (z + RING - step) % RING, (z + step) % RING
        copies = []
        if step < 3 or h == 3:
            part = gbuf.at[up_slab, rows]
            copies.append(send(part, part, r_send.at[step, h], r_recv.at[step, h], up))
        if step < 3 or h == 2:
            part = gbuf.at[down_slab, rows]
            copies.append(send(part, part, l_send.at[step, h], l_recv.at[step, h], down))
        return copies

    hops = []
    for h in range(3):
        lax.fori_loop(firsts[h], firsts[h] + (PART if h < 2 else 2 * PART), arrived, 0)
        hops.append(pass_on(0, h))
    hops = [hops[0] + hops[1], hops[2]]

    take_in(w_waits)
    from_left, from_right = wbuf.at[j_left, low], wbuf.at[j_right, high]
    w_waits = [
        pass_weights(from_left, from_left, 2, right),
        pass_weights(from_right, from_right, 3, left),
        pass_weights(w_in.at[high], wbuf.at[j, high], 4, right),
        pass_weights(w_in.at[low], wbuf.at[j, low], 5, left),
    ]
    to_sibling(from_left, from_left)
    to_sibling(from_right, from_right)

    def take(step):
        for i, h in enumerate((3, 2)):
            take_in(hops[i])
            if step < 3:
                hops[i] = pass_on(step + 1, h)

    def project(offset):
        slab = (z + RING + offset) % RING
        cols = pl.ds(pl.multiple_of(slab * SLAB, SLAB), SLAB)
        weight = wbuf[:, :, cols].reshape(SLAB, SLAB)
        term = dot(weight, gbuf[slab].reshape(SLAB, TOK))
        acc[...] += term
        return 0

    take(0)
    take_in(w_waits)
    for part in (wbuf.at[j_left, high], wbuf.at[j_right, low], wbuf.at[j_far]):
        to_sibling(part, part)
    take(1)
    take_in(s_waits)
    acc[...] = jnp.zeros_like(acc)
    lax.fori_loop(0, 3, lambda i, _: project(i - i // 2 * 3), 0)
    take(2)
    lax.fori_loop(0, 4, lambda i, _: project((2 + i // 2) * (1 - i % 2 * 2)), 0)
    take(3)
    project(4)

    o_waits = []
    for i in range(1, GROUP):
        peer = (j + i) % GROUP
        rows = pl.ds(pl.multiple_of(peer * 64, 64), 64)
        osend[peer] = acc[rows, :].astype(bf16)
        o_waits.append(
            send(osend.at[peer], obuf.at[j], o_send.at[i], o_recv.at[i], at(ctx, z, peer))
        )
    obuf[j] = acc[pl.ds(pl.multiple_of(j * 64, 64), 64), :].astype(bf16)
    take_in(o_waits)
    for i in range(GROUP):
        out_ref[:, i * TOK : (i + 1) * TOK] = obuf[i]

    for copy in unsent:
        copy.wait_send()

    def sent(i, _):
        tile_copy((ctx + i // GROUP) % CTX, (j + i) % GROUP).wait_send()
        return 0

    lax.fori_loop(1, PLANE, sent, 0)


def per_device(query_gate, key_gate, value_proj, filter_taps, out_weight):
    tokens = SEQ // CTX
    split = (CTX, CHAN, tokens)
    dma = pltpu.SemaphoreType.DMA
    return pl.pallas_call(
        layer_kernel,
        out_shape=jax.ShapeDtypeStruct((CTX * CHAN, tokens), bf16),
        in_specs=[pl.BlockSpec(memory_space=pl.ANY)] * 6,
        out_specs=pl.BlockSpec(memory_space=pltpu.VMEM),
        scratch_shapes=[
            pltpu.VMEM(split, bf16),
            pltpu.VMEM(split, bf16),
            pltpu.VMEM(split, bf16),
            pltpu.VMEM((CTX * CHAN, SEQ), bf16),
            pltpu.VMEM((END, 2 * N2), bf16),
            pltpu.VMEM((N1, 2 * N2), f32),
            pltpu.VMEM(split, bf16),
            pltpu.VMEM(split, bf16),
            pltpu.VMEM(split, bf16),
            pltpu.VMEM((N1 * CHAN, N2), f32),
            pltpu.VMEM((N1 * CHAN, N2), f32),
            pltpu.VMEM((N1 * CHAN, N2), f32),
            pltpu.VMEM((CHAN // BATCH, BATCH * N1, 2 * N2), f32),
            pltpu.VMEM((PLANE, CHAN, TOK), bf16),
            pltpu.VMEM((RING, PLANE, CHAN, TOK), bf16),
            pltpu.VMEM((GROUP, 64, D), bf16),
            pltpu.VMEM((SLAB, TOK), f32),
            pltpu.VMEM((GROUP, 64, TOK), bf16),
            pltpu.VMEM((GROUP, 64, TOK), bf16),
            dma((6,)),
            dma((CTX - 1,)), dma((CTX - 1,)), dma((CTX - 1,)), dma((CTX - 1,)),
            dma((6,)), dma((6,)), dma((6,)), dma((6,)),
            dma((PLANE,)), dma((PLANE,)),
            dma((4, 4)), dma((4, 4)), dma((4, 4)), dma((4, 4)),
            dma((GROUP,)), dma((GROUP,)),
        ],
        compiler_params=pltpu.CompilerParams(
            collective_id=0, has_side_effects=True, vmem_limit_bytes=54784 * 1024
        ),
    )(
        query_gate.reshape(split),
        key_gate.reshape(split),
        value_proj.reshape(split),
        filter_taps,
        out_weight.T,
        jnp.asarray(tables()),
    )


def solution(mesh):
    return jax.shard_map(
        per_device,
        mesh=mesh,
        in_specs=(P("ch", "ctx"), P("ch", "ctx"), P("ch", "ctx"), P("ch", None), P(None, "ch")),
        out_specs=P("ch", "ctx"),
        check_vma=False,
    )
```

```python
import jax
import jax.numpy as jnp
import ml_dtypes
import numpy as np
from jax import lax
from jax.experimental import pallas as pl
from jax.experimental.pallas import tpu as pltpu
from jax.sharding import PartitionSpec as P

SEQ = 8192
N1 = 64
N2 = 128
CTX = 4
GROUP = 8
CHAN = 16
BATCH = 8
RING = 8
PLANE = CTX * GROUP
TOK = 256
D = 4096
SLAB = D // RING
PART = PLANE // 4
NEAR = (0, 1, 3, 2)
MESH = pl.DeviceIdType.MESH

bf16 = jnp.bfloat16
f32 = jnp.float32


def two_parts(table):
    high = table.astype(ml_dtypes.bfloat16)
    low = (table - high.astype(np.float64)).astype(ml_dtypes.bfloat16)
    return high, low


def tables():
    root = np.pi / (2 * SEQ)
    n1, k1, n2, k2 = np.arange(N1), np.arange(N1), np.arange(N2), np.arange(N2)
    first = np.exp(1j * (root * N2 * n1[None, :] - 2 * np.pi * k1[:, None] * n1[None, :] / N1))
    twist = np.exp(1j * (root * n2[None, :] - 2 * np.pi * k1[:, None] * n2[None, :] / SEQ))
    second = np.exp(-2j * np.pi * n2[:, None] * k2[None, :] / N2)
    high, low = two_parts(np.concatenate([first.real, first.imag], axis=0))
    stage1 = np.concatenate([high, low], axis=1)
    fwd = two_parts(np.block([[second.real, second.imag], [-second.imag, second.real]]))
    inv = two_parts(np.block([[second.real, -second.imag], [second.imag, second.real]]))
    high, low = two_parts(np.concatenate([first.real.T, first.imag.T], axis=1) / SEQ)
    last = np.concatenate([high, low], axis=1)
    twist2 = two_parts(np.concatenate([twist.real, twist.imag], axis=1))
    stage1 = np.concatenate([stage1, np.zeros_like(stage1)], axis=1)
    return np.concatenate([*fwd, *inv, last, stage1, *twist2], axis=0)


FWD, INV, LAST, STAGE1, TWIST, END = np.cumsum([0, 4 * N2, 4 * N2, N1, 2 * N1, 2 * N1]).tolist()


def dot(a, b):
    return jnp.dot(a, b, preferred_element_type=f32)


def parts_of(x):
    high = x.astype(bf16)
    return high, (x - high.astype(f32)).astype(bf16)


def dot3(x, table_ref):
    high, low = parts_of(x)
    first, second = table_ref[: 2 * N2], table_ref[2 * N2 :]
    return dot(high, first) + (dot(low, first) + dot(high, second))


def spectrum(ref, c0, stage1, tw_re, tw_im, fwd_ref):
    rows = []
    for c in range(BATCH):
        x = ref[pl.ds(c0 + c, N1, stride=CHAN), :].astype(bf16)
        a = dot(stage1, jnp.concatenate([x, x], axis=0))
        re, im = a[:N1], a[N1:]
        rows.append(jnp.concatenate([re * tw_re - im * tw_im, re * tw_im + im * tw_re], axis=1))
    return dot3(jnp.concatenate(rows, axis=0), fwd_ref)


def layer_kernel(
    q_in, k_in, v_in, f_in, w_in, table_in,
    out_ref,
    q_ref, k_ref, v_ref, f_ref, table, tw_ref,
    prod, pbuf, qbuf, sig, filt, conv, fspec, gsend, gbuf, wbuf, acc, osend, obuf,
    load_sem,
    p_send, p_recv, q_send, q_recv, w_send, w_recv, s_send, s_recv,
    g_send, g_recv, r_send, r_recv, l_send, l_recv, o_send, o_recv,
):
    ctx = lax.axis_index("ctx")
    ch = lax.axis_index("ch")
    z, j = ch // GROUP, ch % GROUP
    x, core = j // 2, j % 2
    me = ctx * GROUP + j

    def at(other_ctx, other_z, other_j):
        return (other_ctx, other_z * GROUP + other_j)

    def send(src, dst, send_sem, recv_sem, device):
        copy = pltpu.make_async_remote_copy(
            src_ref=src, dst_ref=dst, send_sem=send_sem, recv_sem=recv_sem,
            device_id=device, device_id_type=MESH,
        )
        copy.start()
        unsent.append(copy)
        unreceived.append(copy)
        return copy

    unsent, unreceived = [], []
    scattered = False

    def take_in(copies):
        for copy in copies:
            copy.wait_recv()
            unreceived[:] = [other for other in unreceived if other is not copy]

    up, down = at(ctx, (z + 1) % RING, j), at(ctx, (z + RING - 1) % RING, j)
    pairs = [
        (k_in, k_ref), (v_in, v_ref), (f_in, f_ref), (table_in, table), (q_in, q_ref),
        (w_in, wbuf.at[j]),
    ]
    loads = [
        pltpu.make_async_copy(src, dst, load_sem.at[i]) for i, (src, dst) in enumerate(pairs)
    ]
    for copy in loads:
        copy.start()
    barrier = pltpu.get_barrier_semaphore()

    def greet(i, _):
        peer = (me + 1 + i) % PLANE
        pl.semaphore_signal(
            barrier, inc=1, device_id=at(peer // GROUP, z, peer % GROUP), device_id_type=MESH
        )
        return 0

    lax.fori_loop(0, PLANE - 1, greet, 0)
    pl.semaphore_signal(barrier, inc=1, device_id=up, device_id_type=MESH)
    pl.semaphore_signal(barrier, inc=1, device_id=down, device_id_type=MESH)

    loads[0].wait()
    loads[1].wait()
    prod[...] = (k_ref[...].astype(f32) * v_ref[...].astype(f32)).astype(bf16)
    pl.semaphore_wait(barrier, PLANE + 1)

    def spread(src, dst, send_sem, recv_sem):
        peers = [(ctx + i) % CTX for i in range(1, CTX)]
        return [
            send(src.at[peer], dst.at[ctx], send_sem.at[i], recv_sem.at[i], at(peer, z, j))
            for i, peer in enumerate(peers)
        ]

    p_waits = spread(prod, pbuf, p_send, p_recv)
    pbuf[ctx] = prod[ctx]

    xr, xl = (x + 1) % 4, (x + 3) % 4
    right, left = at(ctx, z, xr * 2 + core), at(ctx, z, xl * 2 + core)
    sibling = at(ctx, z, x * 2 + 1 - core)
    j_right, j_left, j_far = xr * 2 + core, xl * 2 + core, ((x + 2) % 4) * 2 + core
    low, high = pl.ds(0, 32), pl.ds(32, 32)

    def pass_weights(src, dst, i, device):
        return send(src, dst, w_send.at[i], w_recv.at[i], device)

    s_waits = []

    def to_sibling(src, dst):
        i = len(s_waits)
        s_waits.append(send(src, dst, s_send.at[i], s_recv.at[i], sibling))

    w_waits = [
        pass_weights(w_in.at[low], wbuf.at[j, low], 0, right),
        pass_weights(w_in.at[high], wbuf.at[j, high], 1, left),
    ]
    to_sibling(w_in, wbuf.at[j])
    q_waits = spread(q_in, qbuf, q_send, q_recv)

    for copy in loads[2:]:
        copy.wait()
    qbuf[ctx] = q_ref[ctx]

    own = pl.ds(pl.multiple_of(ctx * CHAN, CHAN), CHAN)

    def widen_filter(i, _):
        for k in range(CTX):
            n = k * 16 + i
            rows = pl.ds(pl.multiple_of(n * CHAN, CHAN), CHAN)
            filt[rows, :] = f_ref[own, pl.ds(pl.multiple_of(n * N2, N2), N2)].astype(f32)
        return 0

    lax.fori_loop(0, 16, widen_filter, 0)
    fwd_ref, inv_ref = table.at[FWD:INV], table.at[INV:LAST]
    stage1 = table[STAGE1:TWIST, : 2 * N1]
    twist = table[TWIST:END, :].astype(f32)
    tw_ref[...] = twist[:N1] + twist[N1:]
    tw_re, tw_im = tw_ref[:, :N2], tw_ref[:, N2:]

    def filter_step(i, _):
        fspec[i] = spectrum(filt, i * BATCH, stage1, tw_re, tw_im, fwd_ref)
        return 0

    lax.fori_loop(0, CHAN // BATCH, filter_step, 0)

    take_in(p_waits)

    def widen_signal(i, _):
        for k in range(CTX):
            rows = pl.ds(pl.multiple_of((k * 16 + i) * CHAN, CHAN), CHAN)
            sig[rows, :] = pbuf[k, :, pl.ds(pl.multiple_of(i * N2, N2), N2)].astype(f32)
        return 0

    lax.fori_loop(0, 16, widen_signal, 0)

    def conv_step(i, _):
        c0 = i * BATCH
        fs = fspec[i]
        ss = spectrum(sig, c0, stage1, tw_re, tw_im, fwd_ref)
        fr, fi, sr, si = fs[:, :N2], fs[:, N2:], ss[:, :N2], ss[:, N2:]
        back = dot3(jnp.concatenate([fr * sr - fi * si, fr * si + fi * sr], axis=1), inv_ref)
        last = table[LAST:STAGE1, :]
        for c in range(BATCH):
            re = back[c * N1 : (c + 1) * N1, :N2]
            im = back[c * N1 : (c + 1) * N1, N2:]
            u = jnp.concatenate([re * tw_re + im * tw_im, im * tw_re - re * tw_im], axis=0)
            high, low = parts_of(u)
            y = dot(last, jnp.concatenate([high, high], axis=0)) + dot(last[:, :N2], low)
            conv[pl.ds(c0 + c, N1, stride=CHAN), :] = y
        return 0

    lax.fori_loop(0, CHAN // BATCH, conv_step, 0)

    take_in(q_waits)
    slot = j * CTX + ctx

    def tile_copy(peer_ctx, peer_j):
        peer = peer_ctx * GROUP + peer_j
        return pltpu.make_async_remote_copy(
            src_ref=gsend.at[peer], dst_ref=gbuf.at[z, slot], send_sem=g_send.at[peer],
            recv_sem=g_recv.at[slot], device_id=at(peer_ctx, z, peer_j), device_id_type=MESH,
        )

    def gated_tile(peer_ctx, peer_j):
        halves = []
        for n in range(2):
            rows = pl.ds(pl.multiple_of((peer_ctx * 16 + peer_j * 2 + n) * CHAN, CHAN), CHAN)
            cols = pl.ds(pl.multiple_of(peer_j * TOK + n * N2, N2), N2)
            halves.append((qbuf[peer_ctx, :, cols].astype(f32) * conv[rows, :]).astype(bf16))
        return jnp.concatenate(halves, axis=1)

    def scatter(i, dx):
        peer_ctx, peer_j = (ctx + i // 2) % CTX, (x + dx) % 4 * 2 + (core + i) % 2
        gsend[peer_ctx * GROUP + peer_j] = gated_tile(peer_ctx, peer_j)
        tile_copy(peer_ctx, peer_j).start()
        return dx

    for dx in NEAR:
        lax.fori_loop(0 if dx else 1, PART, scatter, dx)
    gbuf[z, slot] = gated_tile(ctx, j)
    scattered = True

    def arrived(i, _):
        @pl.when(i != slot)
        def _():
            pltpu.make_async_remote_copy(
                src_ref=gsend.at[0], dst_ref=gbuf.at[z, i], send_sem=g_send.at[0],
                recv_sem=g_recv.at[i], device_id=up, device_id_type=MESH,
            ).wait_recv()

        return 0

    def pass_on(step, h):
        rows = pl.ds((x + 4 - NEAR[h]) % 4 * PART, PART)
        up_slab, down_slab = (z + RING - step) % RING, (z + step) % RING
        ups = downs = None
        if step < 3 or h < 2:
            part = gbuf.at[up_slab, rows]
            ups = send(part, part, r_send.at[step, h], r_recv.at[step, h], up)
        if step < 3 or h >= 2:
            part = gbuf.at[down_slab, rows]
            downs = send(part, part, l_send.at[step, h], l_recv.at[step, h], down)
        return ups, downs

    hops = {}
    for h in range(4):
        first = (x + 4 - NEAR[h]) % 4 * PART
        lax.fori_loop(first, first + PART, arrived, 0)
        hops[0, h] = pass_on(0, h)

    take_in(w_waits)
    from_left, from_right = wbuf.at[j_left, low], wbuf.at[j_right, high]
    w_waits = [
        pass_weights(from_left, from_left, 2, right),
        pass_weights(from_right, from_right, 3, left),
        pass_weights(w_in.at[high], wbuf.at[j, high], 4, right),
        pass_weights(w_in.at[low], wbuf.at[j, low], 5, left),
    ]
    to_sibling(from_left, from_left)
    to_sibling(from_right, from_right)

    def take(step):
        for h in range(4):
            ups, downs = hops[step, h]
            take_in([copy for copy in (ups, downs) if copy is not None])
            if step < 3:
                hops[step + 1, h] = pass_on(step + 1, h)

    def project(offset):
        slab = (z + RING + offset) % RING
        cols = pl.ds(pl.multiple_of(slab * SLAB, SLAB), SLAB)
        weight = wbuf[:, :, cols].reshape(SLAB, SLAB)
        term = dot(weight, gbuf[slab].reshape(SLAB, TOK))
        acc[...] += term
        return 0

    acc[...] = jnp.zeros_like(acc)
    take(0)
    take(1)
    take_in(w_waits)
    for part in (wbuf.at[j_left, high], wbuf.at[j_right, low], wbuf.at[j_far]):
        to_sibling(part, part)
    take(2)
    take_in(s_waits)
    lax.fori_loop(0, 3, lambda i, _: project(i - i // 2 * 3), 0)
    lax.fori_loop(0, 4, lambda i, _: project((2 + i // 2) * (1 - i % 2 * 2)), 0)
    take(3)
    project(4)

    o_waits = []
    for i in range(1, GROUP):
        peer = (j + i) % GROUP
        rows = pl.ds(pl.multiple_of(peer * 64, 64), 64)
        osend[peer] = acc[rows, :].astype(bf16)
        o_waits.append(
            send(osend.at[peer], obuf.at[j], o_send.at[i], o_recv.at[i], at(ctx, z, peer))
        )
    obuf[j] = acc[pl.ds(pl.multiple_of(j * 64, 64), 64), :].astype(bf16)
    take_in(o_waits)
    for i in range(GROUP):
        out_ref[:, i * TOK : (i + 1) * TOK] = obuf[i]

    for copy in unsent:
        copy.wait_send()

    def sent(i, _):
        tile_copy((ctx + i // GROUP) % CTX, (j + i) % GROUP).wait_send()
        return 0

    lax.fori_loop(1, PLANE, sent, 0)


def per_device(query_gate, key_gate, value_proj, filter_taps, out_weight):
    tokens = SEQ // CTX
    split = (CTX, CHAN, tokens)
    dma = pltpu.SemaphoreType.DMA
    return pl.pallas_call(
        layer_kernel,
        out_shape=jax.ShapeDtypeStruct((CTX * CHAN, tokens), bf16),
        in_specs=[pl.BlockSpec(memory_space=pl.ANY)] * 6,
        out_specs=pl.BlockSpec(memory_space=pltpu.VMEM),
        scratch_shapes=[
            pltpu.VMEM(split, bf16),
            pltpu.VMEM(split, bf16),
            pltpu.VMEM(split, bf16),
            pltpu.VMEM((CTX * CHAN, SEQ), bf16),
            pltpu.VMEM((END, 2 * N2), bf16),
            pltpu.VMEM((N1, 2 * N2), f32),
            pltpu.VMEM(split, bf16),
            pltpu.VMEM(split, bf16),
            pltpu.VMEM(split, bf16),
            pltpu.VMEM((N1 * CHAN, N2), f32),
            pltpu.VMEM((N1 * CHAN, N2), f32),
            pltpu.VMEM((N1 * CHAN, N2), f32),
            pltpu.VMEM((CHAN // BATCH, BATCH * N1, 2 * N2), f32),
            pltpu.VMEM((PLANE, CHAN, TOK), bf16),
            pltpu.VMEM((RING, PLANE, CHAN, TOK), bf16),
            pltpu.VMEM((GROUP, 64, D), bf16),
            pltpu.VMEM((SLAB, TOK), f32),
            pltpu.VMEM((GROUP, 64, TOK), bf16),
            pltpu.VMEM((GROUP, 64, TOK), bf16),
            dma((6,)),
            dma((CTX - 1,)), dma((CTX - 1,)), dma((CTX - 1,)), dma((CTX - 1,)),
            dma((6,)), dma((6,)), dma((6,)), dma((6,)),
            dma((PLANE,)), dma((PLANE,)),
            dma((4, 4)), dma((4, 4)), dma((4, 4)), dma((4, 4)),
            dma((GROUP,)), dma((GROUP,)),
        ],
        compiler_params=pltpu.CompilerParams(
            collective_id=0, has_side_effects=True, vmem_limit_bytes=54784 * 1024
        ),
    )(
        query_gate.reshape(split),
        key_gate.reshape(split),
        value_proj.reshape(split),
        filter_taps,
        out_weight.T,
        jnp.asarray(tables()),
    )


def solution(mesh):
    return jax.shard_map(
        per_device,
        mesh=mesh,
        in_specs=(P("ch", "ctx"), P("ch", "ctx"), P("ch", "ctx"), P("ch", None), P(None, "ch")),
        out_specs=P("ch", "ctx"),
        check_vma=False,
    )
```

```python
import jax
import jax.numpy as jnp
import ml_dtypes
import numpy as np
from jax import lax
from jax.experimental import pallas as pl
from jax.experimental.pallas import tpu as pltpu
from jax.sharding import PartitionSpec as P

SEQ = 8192
N1 = 64
N2 = 128
CTX = 4
GROUP = 8
CHAN = 16
BATCH = 8
RING = 8
PLANE = CTX * GROUP
TOK = 256
D = 4096
SLAB = D // RING
PART = PLANE // 4
NEAR = (0, 1, 3, 2)
MESH = pl.DeviceIdType.MESH

bf16 = jnp.bfloat16
f32 = jnp.float32


def two_parts(table):
    high = table.astype(ml_dtypes.bfloat16)
    low = (table - high.astype(np.float64)).astype(ml_dtypes.bfloat16)
    return high, low


def tables():
    root = np.pi / (2 * SEQ)
    n1, k1, n2, k2 = np.arange(N1), np.arange(N1), np.arange(N2), np.arange(N2)
    first = np.exp(1j * (root * N2 * n1[None, :] - 2 * np.pi * k1[:, None] * n1[None, :] / N1))
    twist = np.exp(1j * (root * n2[None, :] - 2 * np.pi * k1[:, None] * n2[None, :] / SEQ))
    second = np.exp(-2j * np.pi * n2[:, None] * k2[None, :] / N2)
    high, low = two_parts(np.concatenate([first.real, first.imag], axis=0))
    stage1 = np.concatenate([high, low], axis=1)
    fwd = two_parts(np.block([[second.real, second.imag], [-second.imag, second.real]]))
    inv = two_parts(np.block([[second.real, -second.imag], [second.imag, second.real]]))
    high, low = two_parts(np.concatenate([first.real.T, first.imag.T], axis=1) / SEQ)
    last = np.concatenate([high, low], axis=1)
    twist2 = two_parts(np.concatenate([twist.real, twist.imag], axis=1))
    stage1 = np.concatenate([stage1, np.zeros_like(stage1)], axis=1)
    return np.concatenate([*fwd, *inv, last, stage1, *twist2], axis=0)


FWD, INV, LAST, STAGE1, TWIST, END = np.cumsum([0, 4 * N2, 4 * N2, N1, 2 * N1, 2 * N1]).tolist()


def dot(a, b):
    return jnp.dot(a, b, preferred_element_type=f32)


def parts_of(x):
    high = x.astype(bf16)
    return high, (x - high.astype(f32)).astype(bf16)


def dot3(x, table_ref):
    high, low = parts_of(x)
    first, second = table_ref[: 2 * N2], table_ref[2 * N2 :]
    return dot(high, first) + (dot(low, first) + dot(high, second))


def spectrum(ref, c0, stage1, tw_re, tw_im, fwd_ref):
    rows = []
    for c in range(BATCH):
        x = ref[pl.ds(c0 + c, N1, stride=CHAN), :].astype(bf16)
        a = dot(stage1, jnp.concatenate([x, x], axis=0))
        re, im = a[:N1], a[N1:]
        rows.append(jnp.concatenate([re * tw_re - im * tw_im, re * tw_im + im * tw_re], axis=1))
    return dot3(jnp.concatenate(rows, axis=0), fwd_ref)


def layer_kernel(
    q_in, k_in, v_in, f_in, w_in, table_in,
    out_ref,
    q_ref, k_ref, v_ref, f_ref, table, tw_ref,
    prod, pbuf, qbuf, sig, filt, conv, fspec, gsend, gbuf, wbuf, acc, osend, obuf,
    load_sem,
    p_send, p_recv, q_send, q_recv, w_send, w_recv, s_send, s_recv,
    g_send, g_recv, r_send, r_recv, l_send, l_recv, o_send, o_recv,
):
    ctx = lax.axis_index("ctx")
    ch = lax.axis_index("ch")
    z, j = ch // GROUP, ch % GROUP
    x, core = j // 2, j % 2
    me = ctx * GROUP + j

    def at(other_ctx, other_z, other_j):
        return (other_ctx, other_z * GROUP + other_j)

    def send(src, dst, send_sem, recv_sem, device):
        copy = pltpu.make_async_remote_copy(
            src_ref=src, dst_ref=dst, send_sem=send_sem, recv_sem=recv_sem,
            device_id=device, device_id_type=MESH,
        )
        copy.start()
        unsent.append(copy)
        unreceived.append(copy)
        return copy

    unsent, unreceived = [], []
    scattered = False

    def take_in(copies):
        for copy in copies:
            copy.wait_recv()
            unreceived[:] = [other for other in unreceived if other is not copy]

    up, down = at(ctx, (z + 1) % RING, j), at(ctx, (z + RING - 1) % RING, j)
    pairs = [
        (k_in, k_ref), (v_in, v_ref), (f_in, f_ref), (table_in, table), (q_in, q_ref),
        (w_in, wbuf.at[j]),
    ]
    loads = [
        pltpu.make_async_copy(src, dst, load_sem.at[i]) for i, (src, dst) in enumerate(pairs)
    ]
    for copy in loads:
        copy.start()
    barrier = pltpu.get_barrier_semaphore()

    def greet(i, _):
        peer = (me + 1 + i) % PLANE
        pl.semaphore_signal(
            barrier, inc=1, device_id=at(peer // GROUP, z, peer % GROUP), device_id_type=MESH
        )
        return 0

    lax.fori_loop(0, PLANE - 1, greet, 0)
    pl.semaphore_signal(barrier, inc=1, device_id=up, device_id_type=MESH)
    pl.semaphore_signal(barrier, inc=1, device_id=down, device_id_type=MESH)

    loads[0].wait()
    loads[1].wait()
    prod[...] = (k_ref[...].astype(f32) * v_ref[...].astype(f32)).astype(bf16)
    pl.semaphore_wait(barrier, PLANE + 1)

    def spread(src, dst, send_sem, recv_sem):
        peers = [(ctx + i) % CTX for i in range(1, CTX)]
        return [
            send(src.at[peer], dst.at[ctx], send_sem.at[i], recv_sem.at[i], at(peer, z, j))
            for i, peer in enumerate(peers)
        ]

    p_waits = spread(prod, pbuf, p_send, p_recv)
    pbuf[ctx] = prod[ctx]

    xr, xl = (x + 1) % 4, (x + 3) % 4
    right, left = at(ctx, z, xr * 2 + core), at(ctx, z, xl * 2 + core)
    sibling = at(ctx, z, x * 2 + 1 - core)
    j_right, j_left, j_far = xr * 2 + core, xl * 2 + core, ((x + 2) % 4) * 2 + core
    low, high = pl.ds(0, 32), pl.ds(32, 32)

    def pass_weights(src, dst, i, device):
        return send(src, dst, w_send.at[i], w_recv.at[i], device)

    s_waits = []

    def to_sibling(src, dst):
        i = len(s_waits)
        s_waits.append(send(src, dst, s_send.at[i], s_recv.at[i], sibling))

    w_waits = [
        pass_weights(w_in.at[low], wbuf.at[j, low], 0, right),
        pass_weights(w_in.at[high], wbuf.at[j, high], 1, left),
    ]
    to_sibling(w_in, wbuf.at[j])
    q_waits = spread(q_in, qbuf, q_send, q_recv)

    for copy in loads[2:]:
        copy.wait()
    qbuf[ctx] = q_ref[ctx]

    own = pl.ds(pl.multiple_of(ctx * CHAN, CHAN), CHAN)

    def widen_filter(i, _):
        for k in range(CTX):
            n = k * 16 + i
            rows = pl.ds(pl.multiple_of(n * CHAN, CHAN), CHAN)
            filt[rows, :] = f_ref[own, pl.ds(pl.multiple_of(n * N2, N2), N2)].astype(f32)
        return 0

    lax.fori_loop(0, 16, widen_filter, 0)
    fwd_ref, inv_ref = table.at[FWD:INV], table.at[INV:LAST]
    stage1 = table[STAGE1:TWIST, : 2 * N1]
    twist = table[TWIST:END, :].astype(f32)
    tw_ref[...] = twist[:N1] + twist[N1:]
    tw_re, tw_im = tw_ref[:, :N2], tw_ref[:, N2:]

    def filter_step(i, _):
        fspec[i] = spectrum(filt, i * BATCH, stage1, tw_re, tw_im, fwd_ref)
        return 0

    lax.fori_loop(0, CHAN // BATCH, filter_step, 0)

    take_in(p_waits)

    def widen_signal(i, _):
        for k in range(CTX):
            rows = pl.ds(pl.multiple_of((k * 16 + i) * CHAN, CHAN), CHAN)
            sig[rows, :] = pbuf[k, :, pl.ds(pl.multiple_of(i * N2, N2), N2)].astype(f32)
        return 0

    lax.fori_loop(0, 16, widen_signal, 0)

    def conv_step(i, _):
        c0 = i * BATCH
        fs = fspec[i]
        ss = spectrum(sig, c0, stage1, tw_re, tw_im, fwd_ref)
        fr, fi, sr, si = fs[:, :N2], fs[:, N2:], ss[:, :N2], ss[:, N2:]
        back = dot3(jnp.concatenate([fr * sr - fi * si, fr * si + fi * sr], axis=1), inv_ref)
        last = table[LAST:STAGE1, :]
        for c in range(BATCH):
            re = back[c * N1 : (c + 1) * N1, :N2]
            im = back[c * N1 : (c + 1) * N1, N2:]
            u = jnp.concatenate([re * tw_re + im * tw_im, im * tw_re - re * tw_im], axis=0)
            high, low = parts_of(u)
            y = dot(last, jnp.concatenate([high, high], axis=0)) + dot(last[:, :N2], low)
            conv[pl.ds(c0 + c, N1, stride=CHAN), :] = y
        return 0

    lax.fori_loop(0, CHAN // BATCH, conv_step, 0)

    take_in(q_waits)
    slot = j * CTX + ctx

    def tile_copy(peer_ctx, peer_j):
        peer = peer_ctx * GROUP + peer_j
        return pltpu.make_async_remote_copy(
            src_ref=gsend.at[peer], dst_ref=gbuf.at[z, slot], send_sem=g_send.at[peer],
            recv_sem=g_recv.at[slot], device_id=at(peer_ctx, z, peer_j), device_id_type=MESH,
        )

    def gated_tile(peer_ctx, peer_j):
        halves = []
        for n in range(2):
            rows = pl.ds(pl.multiple_of((peer_ctx * 16 + peer_j * 2 + n) * CHAN, CHAN), CHAN)
            cols = pl.ds(pl.multiple_of(peer_j * TOK + n * N2, N2), N2)
            halves.append((qbuf[peer_ctx, :, cols].astype(f32) * conv[rows, :]).astype(bf16))
        return jnp.concatenate(halves, axis=1)

    def scatter(i, dx):
        peer_ctx, peer_j = (ctx + i // 2) % CTX, (x + dx) % 4 * 2 + (core + i) % 2
        gsend[peer_ctx * GROUP + peer_j] = gated_tile(peer_ctx, peer_j)
        tile_copy(peer_ctx, peer_j).start()
        return dx

    for dx in NEAR:
        lax.fori_loop(0 if dx else 1, PART, scatter, dx)
    gbuf[z, slot] = gated_tile(ctx, j)
    scattered = True

    def arrived(i, _):
        @pl.when(i != slot)
        def _():
            pltpu.make_async_remote_copy(
                src_ref=gsend.at[0], dst_ref=gbuf.at[z, i], send_sem=g_send.at[0],
                recv_sem=g_recv.at[i], device_id=up, device_id_type=MESH,
            ).wait_recv()

        return 0

    def pass_on(step, h):
        rows = pl.ds((x + 4 - NEAR[h]) % 4 * PART, PART)
        up_slab, down_slab = (z + RING - step) % RING, (z + step) % RING
        ups = downs = None
        if step < 3 or h < 2:
            part = gbuf.at[up_slab, rows]
            ups = send(part, part, r_send.at[step, h], r_recv.at[step, h], up)
        if step < 3 or h >= 2:
            part = gbuf.at[down_slab, rows]
            downs = send(part, part, l_send.at[step, h], l_recv.at[step, h], down)
        return ups, downs

    hops = {}
    for h in range(4):
        first = (x + 4 - NEAR[h]) % 4 * PART
        lax.fori_loop(first, first + PART, arrived, 0)
        hops[0, h] = pass_on(0, h)

    take_in(w_waits)
    from_left, from_right = wbuf.at[j_left, low], wbuf.at[j_right, high]
    w_waits = [
        pass_weights(from_left, from_left, 2, right),
        pass_weights(from_right, from_right, 3, left),
        pass_weights(w_in.at[high], wbuf.at[j, high], 4, right),
        pass_weights(w_in.at[low], wbuf.at[j, low], 5, left),
    ]
    to_sibling(from_left, from_left)
    to_sibling(from_right, from_right)

    def take(step):
        for h in range(4):
            ups, downs = hops[step, h]
            take_in([copy for copy in (ups, downs) if copy is not None])
            if step < 3:
                hops[step + 1, h] = pass_on(step + 1, h)

    def project(offset):
        slab = (z + RING + offset) % RING
        cols = pl.ds(pl.multiple_of(slab * SLAB, SLAB), SLAB)
        weight = wbuf[:, :, cols].reshape(SLAB, SLAB)
        term = dot(weight, gbuf[slab].reshape(SLAB, TOK))
        acc[...] += term
        return 0

    acc[...] = jnp.zeros_like(acc)
    take(0)
    take(1)
    take_in(w_waits)
    for part in (wbuf.at[j_left, high], wbuf.at[j_right, low], wbuf.at[j_far]):
        to_sibling(part, part)
    sends_so_far = len(unsent)
    take(2)
    take_in(s_waits)
    lax.fori_loop(0, 3, lambda i, _: project(i - i // 2 * 3), 0)
    lax.fori_loop(0, 4, lambda i, _: project((2 + i // 2) * (1 - i % 2 * 2)), 0)
    for copy in unsent[:sends_so_far]:
        copy.wait_send()
    del unsent[:sends_so_far]

    def sent(i, _):
        tile_copy((ctx + i // GROUP) % CTX, (j + i) % GROUP).wait_send()
        return 0

    lax.fori_loop(1, PLANE, sent, 0)

    take(3)
    project(4)

    o_waits = []
    for i in range(1, GROUP):
        peer = (j + i) % GROUP
        rows = pl.ds(pl.multiple_of(peer * 64, 64), 64)
        osend[peer] = acc[rows, :].astype(bf16)
        o_waits.append(
            send(osend.at[peer], obuf.at[j], o_send.at[i], o_recv.at[i], at(ctx, z, peer))
        )
    obuf[j] = acc[pl.ds(pl.multiple_of(j * 64, 64), 64), :].astype(bf16)
    out_ref[:, pl.ds(pl.multiple_of(j * TOK, TOK), TOK)] = obuf[j]
    for i, copy in enumerate(o_waits):
        take_in([copy])
        source = (j + GROUP - 1 - i) % GROUP
        out_ref[:, pl.ds(pl.multiple_of(source * TOK, TOK), TOK)] = obuf[source]

    for copy in unsent:
        copy.wait_send()


def per_device(query_gate, key_gate, value_proj, filter_taps, out_weight):
    tokens = SEQ // CTX
    split = (CTX, CHAN, tokens)
    dma = pltpu.SemaphoreType.DMA
    return pl.pallas_call(
        layer_kernel,
        out_shape=jax.ShapeDtypeStruct((CTX * CHAN, tokens), bf16),
        in_specs=[pl.BlockSpec(memory_space=pl.ANY)] * 6,
        out_specs=pl.BlockSpec(memory_space=pltpu.VMEM),
        scratch_shapes=[
            pltpu.VMEM(split, bf16),
            pltpu.VMEM(split, bf16),
            pltpu.VMEM(split, bf16),
            pltpu.VMEM((CTX * CHAN, SEQ), bf16),
            pltpu.VMEM((END, 2 * N2), bf16),
            pltpu.VMEM((N1, 2 * N2), f32),
            pltpu.VMEM(split, bf16),
            pltpu.VMEM(split, bf16),
            pltpu.VMEM(split, bf16),
            pltpu.VMEM((N1 * CHAN, N2), f32),
            pltpu.VMEM((N1 * CHAN, N2), f32),
            pltpu.VMEM((N1 * CHAN, N2), f32),
            pltpu.VMEM((CHAN // BATCH, BATCH * N1, 2 * N2), f32),
            pltpu.VMEM((PLANE, CHAN, TOK), bf16),
            pltpu.VMEM((RING, PLANE, CHAN, TOK), bf16),
            pltpu.VMEM((GROUP, 64, D), bf16),
            pltpu.VMEM((SLAB, TOK), f32),
            pltpu.VMEM((GROUP, 64, TOK), bf16),
            pltpu.VMEM((GROUP, 64, TOK), bf16),
            dma((6,)),
            dma((CTX - 1,)), dma((CTX - 1,)), dma((CTX - 1,)), dma((CTX - 1,)),
            dma((6,)), dma((6,)), dma((6,)), dma((6,)),
            dma((PLANE,)), dma((PLANE,)),
            dma((4, 4)), dma((4, 4)), dma((4, 4)), dma((4, 4)),
            dma((GROUP,)), dma((GROUP,)),
        ],
        compiler_params=pltpu.CompilerParams(
            collective_id=0, has_side_effects=True, vmem_limit_bytes=54784 * 1024
        ),
    )(
        query_gate.reshape(split),
        key_gate.reshape(split),
        value_proj.reshape(split),
        filter_taps,
        out_weight.T,
        jnp.asarray(tables()),
    )


def solution(mesh):
    return jax.shard_map(
        per_device,
        mesh=mesh,
        in_specs=(P("ch", "ctx"), P("ch", "ctx"), P("ch", "ctx"), P("ch", None), P(None, "ch")),
        out_specs=P("ch", "ctx"),
        check_vma=False,
    )
```

```python
import jax
import jax.numpy as jnp
import ml_dtypes
import numpy as np
from jax import lax
from jax.experimental import pallas as pl
from jax.experimental.pallas import tpu as pltpu
from jax.sharding import PartitionSpec as P

SEQ = 8192
N1 = 64
N2 = 128
CTX = 4
GROUP = 8
CHAN = 16
BATCH = 16
RING = 8
PLANE = CTX * GROUP
TOK = 256
D = 4096
SLAB = D // RING
PART = PLANE // 4
NEAR = (0, 1, 3, 2)
MESH = pl.DeviceIdType.MESH

bf16 = jnp.bfloat16
f32 = jnp.float32


def two_parts(table):
    high = table.astype(ml_dtypes.bfloat16)
    low = (table - high.astype(np.float64)).astype(ml_dtypes.bfloat16)
    return high, low


def tables():
    root = np.pi / (2 * SEQ)
    n1, k1, n2, k2 = np.arange(N1), np.arange(N1), np.arange(N2), np.arange(N2)
    first = np.exp(1j * (root * N2 * n1[None, :] - 2 * np.pi * k1[:, None] * n1[None, :] / N1))
    twist = np.exp(1j * (root * n2[None, :] - 2 * np.pi * k1[:, None] * n2[None, :] / SEQ))
    second = np.exp(-2j * np.pi * n2[:, None] * k2[None, :] / N2)
    high, low = two_parts(np.concatenate([first.real, first.imag], axis=0))
    stage1 = np.concatenate([high, low], axis=1)
    fwd = two_parts(np.block([[second.real, second.imag], [-second.imag, second.real]]))
    inv = two_parts(np.block([[second.real, -second.imag], [second.imag, second.real]]))
    high, low = two_parts(np.concatenate([first.real.T, first.imag.T], axis=1) / SEQ)
    last = np.concatenate([high, low], axis=1)
    twist2 = two_parts(np.concatenate([twist.real, twist.imag], axis=1))
    stage1 = np.concatenate([stage1, np.zeros_like(stage1)], axis=1)
    return np.concatenate([*fwd, *inv, last, stage1, *twist2], axis=0)


FWD, INV, LAST, STAGE1, TWIST, END = np.cumsum([0, 4 * N2, 4 * N2, N1, 2 * N1, 2 * N1]).tolist()


def dot(a, b):
    return jnp.dot(a, b, preferred_element_type=f32)


def parts_of(x):
    high = x.astype(bf16)
    return high, (x - high.astype(f32)).astype(bf16)


def dot3(x, table_ref):
    high, low = parts_of(x)
    first, second = table_ref[: 2 * N2], table_ref[2 * N2 :]
    return dot(high, first) + (dot(low, first) + dot(high, second))


def spectrum(ref, c0, stage1, tw_re, tw_im, fwd_ref):
    rows = []
    for c in range(BATCH):
        x = ref[pl.ds(c0 + c, N1, stride=CHAN), :].astype(bf16)
        a = dot(stage1, jnp.concatenate([x, x], axis=0))
        re, im = a[:N1], a[N1:]
        rows.append(jnp.concatenate([re * tw_re - im * tw_im, re * tw_im + im * tw_re], axis=1))
    return dot3(jnp.concatenate(rows, axis=0), fwd_ref)


def layer_kernel(
    q_in, k_in, v_in, f_in, w_in, table_in,
    out_ref,
    q_ref, k_ref, v_ref, f_ref, table, tw_ref,
    prod, pbuf, qbuf, sig, filt, conv, fspec, gsend, gbuf, wbuf, acc, osend, obuf,
    load_sem,
    p_send, p_recv, q_send, q_recv, w_send, w_recv, s_send, s_recv,
    g_send, g_recv, r_send, r_recv, l_send, l_recv, o_send, o_recv,
):
    ctx = lax.axis_index("ctx")
    ch = lax.axis_index("ch")
    z, j = ch // GROUP, ch % GROUP
    x, core = j // 2, j % 2
    me = ctx * GROUP + j

    def at(other_ctx, other_z, other_j):
        return (other_ctx, other_z * GROUP + other_j)

    def send(src, dst, send_sem, recv_sem, device):
        copy = pltpu.make_async_remote_copy(
            src_ref=src, dst_ref=dst, send_sem=send_sem, recv_sem=recv_sem,
            device_id=device, device_id_type=MESH,
        )
        copy.start()
        unsent.append(copy)
        unreceived.append(copy)
        return copy

    unsent, unreceived = [], []
    scattered = False

    def take_in(copies):
        for copy in copies:
            copy.wait_recv()
            unreceived[:] = [other for other in unreceived if other is not copy]

    up, down = at(ctx, (z + 1) % RING, j), at(ctx, (z + RING - 1) % RING, j)
    pairs = [
        (k_in, k_ref), (v_in, v_ref), (f_in, f_ref), (table_in, table), (q_in, q_ref),
        (w_in, wbuf.at[j]),
    ]
    loads = [
        pltpu.make_async_copy(src, dst, load_sem.at[i]) for i, (src, dst) in enumerate(pairs)
    ]
    for copy in loads:
        copy.start()
    barrier = pltpu.get_barrier_semaphore()

    def greet(i, _):
        peer = (me + 1 + i) % PLANE
        pl.semaphore_signal(
            barrier, inc=1, device_id=at(peer // GROUP, z, peer % GROUP), device_id_type=MESH
        )
        return 0

    lax.fori_loop(0, PLANE - 1, greet, 0)
    pl.semaphore_signal(barrier, inc=1, device_id=up, device_id_type=MESH)
    pl.semaphore_signal(barrier, inc=1, device_id=down, device_id_type=MESH)

    loads[0].wait()
    loads[1].wait()
    prod[...] = (k_ref[...].astype(f32) * v_ref[...].astype(f32)).astype(bf16)
    pl.semaphore_wait(barrier, PLANE + 1)

    def spread(src, dst, send_sem, recv_sem):
        peers = [(ctx + i) % CTX for i in range(1, CTX)]
        return [
            send(src.at[peer], dst.at[ctx], send_sem.at[i], recv_sem.at[i], at(peer, z, j))
            for i, peer in enumerate(peers)
        ]

    p_waits = spread(prod, pbuf, p_send, p_recv)
    pbuf[ctx] = prod[ctx]

    xr, xl = (x + 1) % 4, (x + 3) % 4
    right, left = at(ctx, z, xr * 2 + core), at(ctx, z, xl * 2 + core)
    sibling = at(ctx, z, x * 2 + 1 - core)
    j_right, j_left, j_far = xr * 2 + core, xl * 2 + core, ((x + 2) % 4) * 2 + core
    low, high = pl.ds(0, 32), pl.ds(32, 32)

    def pass_weights(src, dst, i, device):
        return send(src, dst, w_send.at[i], w_recv.at[i], device)

    s_waits = []

    def to_sibling(src, dst):
        i = len(s_waits)
        s_waits.append(send(src, dst, s_send.at[i], s_recv.at[i], sibling))

    w_waits = [
        pass_weights(w_in.at[low], wbuf.at[j, low], 0, right),
        pass_weights(w_in.at[high], wbuf.at[j, high], 1, left),
    ]
    to_sibling(w_in, wbuf.at[j])

    for copy in loads[2:]:
        copy.wait()
    qbuf[ctx] = q_ref[ctx]

    own = pl.ds(pl.multiple_of(ctx * CHAN, CHAN), CHAN)

    def widen_filter(i, _):
        for k in range(CTX):
            n = k * 16 + i
            rows = pl.ds(pl.multiple_of(n * CHAN, CHAN), CHAN)
            filt[rows, :] = f_ref[own, pl.ds(pl.multiple_of(n * N2, N2), N2)].astype(f32)
        return 0

    lax.fori_loop(0, 16, widen_filter, 0)
    fwd_ref, inv_ref = table.at[FWD:INV], table.at[INV:LAST]
    stage1 = table[STAGE1:TWIST, : 2 * N1]
    twist = table[TWIST:END, :].astype(f32)
    tw_ref[...] = twist[:N1] + twist[N1:]
    tw_re, tw_im = tw_ref[:, :N2], tw_ref[:, N2:]

    def filter_step(i, _):
        fspec[i] = spectrum(filt, i * BATCH, stage1, tw_re, tw_im, fwd_ref)
        return 0

    lax.fori_loop(0, CHAN // BATCH, filter_step, 0)
    q_waits = spread(q_in, qbuf, q_send, q_recv)


    def widen_signal(i, part):
        for k in range(4):
            n = i * 4 + k
            rows = pl.ds(pl.multiple_of((part * 16 + n) * CHAN, CHAN), CHAN)
            sig[rows, :] = pbuf[part, :, pl.ds(pl.multiple_of(n * N2, N2), N2)].astype(f32)
        return part

    lax.fori_loop(0, 4, widen_signal, ctx)
    for i in (0, 2, 1):
        take_in([p_waits[i]])
        lax.fori_loop(0, 4, widen_signal, (ctx + CTX - 1 - i) % CTX)

    def conv_step(i, _):
        c0 = i * BATCH
        fs = fspec[i]
        ss = spectrum(sig, c0, stage1, tw_re, tw_im, fwd_ref)
        fr, fi, sr, si = fs[:, :N2], fs[:, N2:], ss[:, :N2], ss[:, N2:]
        back = dot3(jnp.concatenate([fr * sr - fi * si, fr * si + fi * sr], axis=1), inv_ref)
        last = table[LAST:STAGE1, :]
        for c in range(BATCH):
            re = back[c * N1 : (c + 1) * N1, :N2]
            im = back[c * N1 : (c + 1) * N1, N2:]
            u = jnp.concatenate([re * tw_re + im * tw_im, im * tw_re - re * tw_im], axis=0)
            high, low = parts_of(u)
            y = dot(last, jnp.concatenate([high, high], axis=0)) + dot(last[:, :N2], low)
            conv[pl.ds(c0 + c, N1, stride=CHAN), :] = y
        return 0

    lax.fori_loop(0, CHAN // BATCH, conv_step, 0)

    take_in(q_waits)
    slot = j * CTX + ctx

    def tile_copy(peer_ctx, peer_j):
        peer = peer_ctx * GROUP + peer_j
        return pltpu.make_async_remote_copy(
            src_ref=gsend.at[peer], dst_ref=gbuf.at[z, slot], send_sem=g_send.at[peer],
            recv_sem=g_recv.at[slot], device_id=at(peer_ctx, z, peer_j), device_id_type=MESH,
        )

    def gated_tile(peer_ctx, peer_j):
        halves = []
        for n in range(2):
            rows = pl.ds(pl.multiple_of((peer_ctx * 16 + peer_j * 2 + n) * CHAN, CHAN), CHAN)
            cols = pl.ds(pl.multiple_of(peer_j * TOK + n * N2, N2), N2)
            halves.append((qbuf[peer_ctx, :, cols].astype(f32) * conv[rows, :]).astype(bf16))
        return jnp.concatenate(halves, axis=1)

    def scatter(i, dx):
        peer_ctx, peer_j = (ctx + i // 2) % CTX, (x + dx) % 4 * 2 + (core + i) % 2
        gsend[peer_ctx * GROUP + peer_j] = gated_tile(peer_ctx, peer_j)
        tile_copy(peer_ctx, peer_j).start()
        return dx

    for dx in NEAR:
        lax.fori_loop(0 if dx else 1, PART, scatter, dx)
    gbuf[z, slot] = gated_tile(ctx, j)
    scattered = True

    def arrived(i, _):
        @pl.when(i != slot)
        def _():
            pltpu.make_async_remote_copy(
                src_ref=gsend.at[0], dst_ref=gbuf.at[z, i], send_sem=g_send.at[0],
                recv_sem=g_recv.at[i], device_id=up, device_id_type=MESH,
            ).wait_recv()

        return 0

    def pass_on(step, h):
        rows = pl.ds((x + 4 - NEAR[h]) % 4 * PART, PART)
        up_slab, down_slab = (z + RING - step) % RING, (z + step) % RING
        ups = downs = None
        if step < 3 or h < 2:
            part = gbuf.at[up_slab, rows]
            ups = send(part, part, r_send.at[step, h], r_recv.at[step, h], up)
        if step < 3 or h >= 2:
            part = gbuf.at[down_slab, rows]
            downs = send(part, part, l_send.at[step, h], l_recv.at[step, h], down)
        return ups, downs

    hops = {}
    for h in range(4):
        first = (x + 4 - NEAR[h]) % 4 * PART
        lax.fori_loop(first, first + PART, arrived, 0)
        hops[0, h] = pass_on(0, h)

    take_in(w_waits)
    from_left, from_right = wbuf.at[j_left, low], wbuf.at[j_right, high]
    w_waits = [
        pass_weights(from_left, from_left, 2, right),
        pass_weights(from_right, from_right, 3, left),
        pass_weights(w_in.at[high], wbuf.at[j, high], 4, right),
        pass_weights(w_in.at[low], wbuf.at[j, low], 5, left),
    ]
    to_sibling(from_left, from_left)
    to_sibling(from_right, from_right)

    def take(step):
        for h in range(4):
            ups, downs = hops[step, h]
            take_in([copy for copy in (ups, downs) if copy is not None])
            if step < 3:
                hops[step + 1, h] = pass_on(step + 1, h)

    def project(offset):
        slab = (z + RING + offset) % RING
        cols = pl.ds(pl.multiple_of(slab * SLAB, SLAB), SLAB)
        weight = wbuf[:, :, cols].reshape(SLAB, SLAB)
        term = dot(weight, gbuf[slab].reshape(SLAB, TOK))
        acc[...] += term
        return 0

    acc[...] = jnp.zeros_like(acc)
    take(0)
    take(1)
    take_in(w_waits)
    for part in (wbuf.at[j_left, high], wbuf.at[j_right, low], wbuf.at[j_far]):
        to_sibling(part, part)
    sends_so_far = len(unsent)
    take(2)
    take_in(s_waits)
    lax.fori_loop(0, 3, lambda i, _: project(i - i // 2 * 3), 0)
    lax.fori_loop(0, 4, lambda i, _: project((2 + i // 2) * (1 - i % 2 * 2)), 0)
    for copy in unsent[:sends_so_far]:
        copy.wait_send()
    del unsent[:sends_so_far]

    def sent(i, _):
        tile_copy((ctx + i // GROUP) % CTX, (j + i) % GROUP).wait_send()
        return 0

    lax.fori_loop(1, PLANE, sent, 0)

    take(3)
    project(4)

    o_waits = []
    for i in range(1, GROUP):
        peer = (j + i) % GROUP
        rows = pl.ds(pl.multiple_of(peer * 64, 64), 64)
        osend[peer] = acc[rows, :].astype(bf16)
        o_waits.append(
            send(osend.at[peer], obuf.at[j], o_send.at[i], o_recv.at[i], at(ctx, z, peer))
        )
    obuf[j] = acc[pl.ds(pl.multiple_of(j * 64, 64), 64), :].astype(bf16)
    out_ref[:, pl.ds(pl.multiple_of(j * TOK, TOK), TOK)] = obuf[j]
    for i, copy in enumerate(o_waits):
        take_in([copy])
        source = (j + GROUP - 1 - i) % GROUP
        out_ref[:, pl.ds(pl.multiple_of(source * TOK, TOK), TOK)] = obuf[source]

    for copy in unsent:
        copy.wait_send()


def per_device(query_gate, key_gate, value_proj, filter_taps, out_weight):
    tokens = SEQ // CTX
    split = (CTX, CHAN, tokens)
    dma = pltpu.SemaphoreType.DMA
    return pl.pallas_call(
        layer_kernel,
        out_shape=jax.ShapeDtypeStruct((CTX * CHAN, tokens), bf16),
        in_specs=[pl.BlockSpec(memory_space=pl.ANY)] * 6,
        out_specs=pl.BlockSpec(memory_space=pltpu.VMEM),
        scratch_shapes=[
            pltpu.VMEM(split, bf16),
            pltpu.VMEM(split, bf16),
            pltpu.VMEM(split, bf16),
            pltpu.VMEM((CTX * CHAN, SEQ), bf16),
            pltpu.VMEM((END, 2 * N2), bf16),
            pltpu.VMEM((N1, 2 * N2), f32),
            pltpu.VMEM(split, bf16),
            pltpu.VMEM(split, bf16),
            pltpu.VMEM(split, bf16),
            pltpu.VMEM((N1 * CHAN, N2), f32),
            pltpu.VMEM((N1 * CHAN, N2), f32),
            pltpu.VMEM((N1 * CHAN, N2), f32),
            pltpu.VMEM((CHAN // BATCH, BATCH * N1, 2 * N2), f32),
            pltpu.VMEM((PLANE, CHAN, TOK), bf16),
            pltpu.VMEM((RING, PLANE, CHAN, TOK), bf16),
            pltpu.VMEM((GROUP, 64, D), bf16),
            pltpu.VMEM((SLAB, TOK), f32),
            pltpu.VMEM((GROUP, 64, TOK), bf16),
            pltpu.VMEM((GROUP, 64, TOK), bf16),
            dma((6,)),
            dma((CTX - 1,)), dma((CTX - 1,)), dma((CTX - 1,)), dma((CTX - 1,)),
            dma((6,)), dma((6,)), dma((6,)), dma((6,)),
            dma((PLANE,)), dma((PLANE,)),
            dma((4, 4)), dma((4, 4)), dma((4, 4)), dma((4, 4)),
            dma((GROUP,)), dma((GROUP,)),
        ],
        compiler_params=pltpu.CompilerParams(
            collective_id=0, has_side_effects=True, vmem_limit_bytes=54784 * 1024
        ),
    )(
        query_gate.reshape(split),
        key_gate.reshape(split),
        value_proj.reshape(split),
        filter_taps,
        out_weight.T,
        jnp.asarray(tables()),
    )


def solution(mesh):
    return jax.shard_map(
        per_device,
        mesh=mesh,
        in_specs=(P("ch", "ctx"), P("ch", "ctx"), P("ch", "ctx"), P("ch", None), P(None, "ch")),
        out_specs=P("ch", "ctx"),
        check_vma=False,
    )
```

```python
import jax
import jax.numpy as jnp
import ml_dtypes
import numpy as np
from jax import lax
from jax.experimental import pallas as pl
from jax.experimental.pallas import tpu as pltpu
from jax.sharding import PartitionSpec as P

SEQ = 8192
N1 = 64
N2 = 128
CTX = 4
GROUP = 8
CHAN = 16
BATCH = 16
RING = 8
PLANE = CTX * GROUP
TOK = 256
D = 4096
SLAB = D // RING
PART = PLANE // 4
NEAR = (0, 1, 3, 2)
MESH = pl.DeviceIdType.MESH

bf16 = jnp.bfloat16
f32 = jnp.float32


def two_parts(table):
    high = table.astype(ml_dtypes.bfloat16)
    low = (table - high.astype(np.float64)).astype(ml_dtypes.bfloat16)
    return high, low


def tables():
    root = np.pi / (2 * SEQ)
    n1, k1, n2, k2 = np.arange(N1), np.arange(N1), np.arange(N2), np.arange(N2)
    first = np.exp(1j * (root * N2 * n1[None, :] - 2 * np.pi * k1[:, None] * n1[None, :] / N1))
    twist = np.exp(1j * (root * n2[None, :] - 2 * np.pi * k1[:, None] * n2[None, :] / SEQ))
    second = np.exp(-2j * np.pi * n2[:, None] * k2[None, :] / N2)
    high, low = two_parts(np.concatenate([first.real, first.imag], axis=0))
    stage1 = np.concatenate([high, low], axis=1)
    fwd = two_parts(np.block([[second.real, second.imag], [-second.imag, second.real]]))
    inv = two_parts(np.block([[second.real, -second.imag], [second.imag, second.real]]))
    high, low = two_parts(np.concatenate([first.real.T, first.imag.T], axis=1) / SEQ)
    last = np.concatenate([high, low], axis=1)
    twist2 = two_parts(np.concatenate([twist.real, twist.imag], axis=1))
    stage1 = np.concatenate([stage1, np.zeros_like(stage1)], axis=1)
    return np.concatenate([*fwd, *inv, last, stage1, *twist2], axis=0)


FWD, INV, LAST, STAGE1, TWIST, END = np.cumsum([0, 4 * N2, 4 * N2, N1, 2 * N1, 2 * N1]).tolist()


def dot(a, b):
    return jnp.dot(a, b, preferred_element_type=f32)


def parts_of(x):
    high = x.astype(bf16)
    return high, (x - high.astype(f32)).astype(bf16)


def dot3(x, table_ref):
    high, low = parts_of(x)
    first, second = table_ref[: 2 * N2], table_ref[2 * N2 :]
    rows = x.shape[0]
    both = dot(jnp.concatenate([high, low], axis=0), first)
    return both[:rows] + (both[rows:] + dot(high, second))


def spectrum(ref, c0, stage1, tw_re, tw_im, fwd_ref):
    rows = []
    for c in range(BATCH):
        x = ref[pl.ds(c0 + c, N1, stride=CHAN), :].astype(bf16)
        a = dot(stage1, jnp.concatenate([x, x], axis=0))
        re, im = a[:N1], a[N1:]
        rows.append(jnp.concatenate([re * tw_re - im * tw_im, re * tw_im + im * tw_re], axis=1))
    return dot3(jnp.concatenate(rows, axis=0), fwd_ref)


def layer_kernel(
    q_in, k_in, v_in, f_in, w_in, table_in,
    out_ref,
    q_ref, k_ref, v_ref, f_ref, table, tw_ref,
    prod, pbuf, qbuf, sig, filt, conv, fspec, gsend, gbuf, wbuf, acc, osend, obuf,
    load_sem,
    p_send, p_recv, q_send, q_recv, w_send, w_recv, s_send, s_recv,
    g_send, g_recv, r_send, r_recv, l_send, l_recv, o_send, o_recv,
):
    ctx = lax.axis_index("ctx")
    ch = lax.axis_index("ch")
    z, j = ch // GROUP, ch % GROUP
    x, core = j // 2, j % 2
    me = ctx * GROUP + j

    def at(other_ctx, other_z, other_j):
        return (other_ctx, other_z * GROUP + other_j)

    def send(src, dst, send_sem, recv_sem, device):
        copy = pltpu.make_async_remote_copy(
            src_ref=src, dst_ref=dst, send_sem=send_sem, recv_sem=recv_sem,
            device_id=device, device_id_type=MESH,
        )
        copy.start()
        unsent.append(copy)
        unreceived.append(copy)
        return copy

    unsent, unreceived = [], []
    scattered = False

    def take_in(copies):
        for copy in copies:
            copy.wait_recv()
            unreceived[:] = [other for other in unreceived if other is not copy]

    up, down = at(ctx, (z + 1) % RING, j), at(ctx, (z + RING - 1) % RING, j)
    pairs = [
        (k_in, k_ref), (v_in, v_ref), (f_in, f_ref), (table_in, table), (q_in, q_ref),
        (w_in, wbuf.at[j]),
    ]
    loads = [
        pltpu.make_async_copy(src, dst, load_sem.at[i]) for i, (src, dst) in enumerate(pairs)
    ]
    for copy in loads:
        copy.start()
    barrier = pltpu.get_barrier_semaphore()

    def greet(i, _):
        peer = (me + 1 + i) % PLANE
        pl.semaphore_signal(
            barrier, inc=1, device_id=at(peer // GROUP, z, peer % GROUP), device_id_type=MESH
        )
        return 0

    lax.fori_loop(0, PLANE - 1, greet, 0, unroll=True)
    pl.semaphore_signal(barrier, inc=1, device_id=up, device_id_type=MESH)
    pl.semaphore_signal(barrier, inc=1, device_id=down, device_id_type=MESH)

    loads[0].wait()
    loads[1].wait()
    prod[...] = (k_ref[...].astype(f32) * v_ref[...].astype(f32)).astype(bf16)
    pl.semaphore_wait(barrier, PLANE + 1)

    def spread(src, dst, send_sem, recv_sem):
        peers = [(ctx + i) % CTX for i in range(1, CTX)]
        return [
            send(src.at[peer], dst.at[ctx], send_sem.at[i], recv_sem.at[i], at(peer, z, j))
            for i, peer in enumerate(peers)
        ]

    p_waits = spread(prod, pbuf, p_send, p_recv)
    pbuf[ctx] = prod[ctx]

    xr, xl = (x + 1) % 4, (x + 3) % 4
    right, left = at(ctx, z, xr * 2 + core), at(ctx, z, xl * 2 + core)
    sibling = at(ctx, z, x * 2 + 1 - core)
    j_right, j_left, j_far = xr * 2 + core, xl * 2 + core, ((x + 2) % 4) * 2 + core
    low, high = pl.ds(0, 32), pl.ds(32, 32)

    def pass_weights(src, dst, i, device):
        return send(src, dst, w_send.at[i], w_recv.at[i], device)

    s_waits = []

    def to_sibling(src, dst):
        i = len(s_waits)
        s_waits.append(send(src, dst, s_send.at[i], s_recv.at[i], sibling))

    w_waits = [
        pass_weights(w_in.at[low], wbuf.at[j, low], 0, right),
        pass_weights(w_in.at[high], wbuf.at[j, high], 1, left),
    ]
    to_sibling(w_in, wbuf.at[j])

    for copy in loads[2:]:
        copy.wait()
    qbuf[ctx] = q_ref[ctx]

    own = pl.ds(pl.multiple_of(ctx * CHAN, CHAN), CHAN)

    def widen_filter(i, _):
        for k in range(CTX):
            n = k * 16 + i
            rows = pl.ds(pl.multiple_of(n * CHAN, CHAN), CHAN)
            filt[rows, :] = f_ref[own, pl.ds(pl.multiple_of(n * N2, N2), N2)].astype(f32)
        return 0

    lax.fori_loop(0, 16, widen_filter, 0)
    fwd_ref, inv_ref = table.at[FWD:INV], table.at[INV:LAST]
    stage1 = table[STAGE1:TWIST, : 2 * N1]
    twist = table[TWIST:END, :].astype(f32)
    tw_ref[...] = twist[:N1] + twist[N1:]
    tw_re, tw_im = tw_ref[:, :N2], tw_ref[:, N2:]

    def filter_step(i, _):
        fspec[i] = spectrum(filt, i * BATCH, stage1, tw_re, tw_im, fwd_ref)
        return 0

    lax.fori_loop(0, CHAN // BATCH, filter_step, 0)
    q_waits = spread(q_in, qbuf, q_send, q_recv)


    def widen_signal(i, part):
        for k in range(4):
            n = i * 4 + k
            rows = pl.ds(pl.multiple_of((part * 16 + n) * CHAN, CHAN), CHAN)
            sig[rows, :] = pbuf[part, :, pl.ds(pl.multiple_of(n * N2, N2), N2)].astype(f32)
        return part

    lax.fori_loop(0, 4, widen_signal, ctx)
    for i in (0, 2, 1):
        take_in([p_waits[i]])
        lax.fori_loop(0, 4, widen_signal, (ctx + CTX - 1 - i) % CTX)

    def conv_step(i, _):
        c0 = i * BATCH
        fs = fspec[i]
        ss = spectrum(sig, c0, stage1, tw_re, tw_im, fwd_ref)
        fr, fi, sr, si = fs[:, :N2], fs[:, N2:], ss[:, :N2], ss[:, N2:]
        back = dot3(jnp.concatenate([fr * sr - fi * si, fr * si + fi * sr], axis=1), inv_ref)
        last = table[LAST:STAGE1, :]
        for c in range(BATCH):
            re = back[c * N1 : (c + 1) * N1, :N2]
            im = back[c * N1 : (c + 1) * N1, N2:]
            u = jnp.concatenate([re * tw_re + im * tw_im, im * tw_re - re * tw_im], axis=0)
            high, low = parts_of(u)
            y = dot(last, jnp.concatenate([high, high], axis=0)) + dot(last[:, :N2], low)
            conv[pl.ds(c0 + c, N1, stride=CHAN), :] = y
        return 0

    lax.fori_loop(0, CHAN // BATCH, conv_step, 0)

    take_in(q_waits)
    slot = j * CTX + ctx

    def tile_copy(peer_ctx, peer_j):
        peer = peer_ctx * GROUP + peer_j
        return pltpu.make_async_remote_copy(
            src_ref=gsend.at[peer], dst_ref=gbuf.at[z, slot], send_sem=g_send.at[peer],
            recv_sem=g_recv.at[slot], device_id=at(peer_ctx, z, peer_j), device_id_type=MESH,
        )

    def gated_tile(peer_ctx, peer_j):
        halves = []
        for n in range(2):
            rows = pl.ds(pl.multiple_of((peer_ctx * 16 + peer_j * 2 + n) * CHAN, CHAN), CHAN)
            cols = pl.ds(pl.multiple_of(peer_j * TOK + n * N2, N2), N2)
            halves.append((qbuf[peer_ctx, :, cols].astype(f32) * conv[rows, :]).astype(bf16))
        return jnp.concatenate(halves, axis=1)

    def scatter(i, dx):
        peer_ctx, peer_j = (ctx + i // 2) % CTX, (x + dx) % 4 * 2 + (core + i) % 2
        gsend[peer_ctx * GROUP + peer_j] = gated_tile(peer_ctx, peer_j)
        tile_copy(peer_ctx, peer_j).start()
        return dx

    for dx in NEAR:
        lax.fori_loop(0 if dx else 1, PART, scatter, dx)
    gbuf[z, slot] = gated_tile(ctx, j)
    scattered = True

    def arrived(i, _):
        @pl.when(i != slot)
        def _():
            pltpu.make_async_remote_copy(
                src_ref=gsend.at[0], dst_ref=gbuf.at[z, i], send_sem=g_send.at[0],
                recv_sem=g_recv.at[i], device_id=up, device_id_type=MESH,
            ).wait_recv()

        return 0

    def pass_on(step, h):
        rows = pl.ds((x + 4 - NEAR[h]) % 4 * PART, PART)
        up_slab, down_slab = (z + RING - step) % RING, (z + step) % RING
        ups = downs = None
        if step < 3 or h < 2:
            part = gbuf.at[up_slab, rows]
            ups = send(part, part, r_send.at[step, h], r_recv.at[step, h], up)
        if step < 3 or h >= 2:
            part = gbuf.at[down_slab, rows]
            downs = send(part, part, l_send.at[step, h], l_recv.at[step, h], down)
        return ups, downs

    hops = {}
    for h in range(4):
        first = (x + 4 - NEAR[h]) % 4 * PART
        lax.fori_loop(first, first + PART, arrived, 0)
        hops[0, h] = pass_on(0, h)

    take_in(w_waits)
    from_left, from_right = wbuf.at[j_left, low], wbuf.at[j_right, high]
    w_waits = [
        pass_weights(from_left, from_left, 2, right),
        pass_weights(from_right, from_right, 3, left),
        pass_weights(w_in.at[high], wbuf.at[j, high], 4, right),
        pass_weights(w_in.at[low], wbuf.at[j, low], 5, left),
    ]
    to_sibling(from_left, from_left)
    to_sibling(from_right, from_right)

    def take(step):
        for h in range(4):
            ups, downs = hops[step, h]
            take_in([copy for copy in (ups, downs) if copy is not None])
            if step < 3:
                hops[step + 1, h] = pass_on(step + 1, h)

    def project(offset):
        slab = (z + RING + offset) % RING
        cols = pl.ds(pl.multiple_of(slab * SLAB, SLAB), SLAB)
        weight = wbuf[:, :, cols].reshape(SLAB, SLAB)
        term = dot(weight, gbuf[slab].reshape(SLAB, TOK))
        acc[...] += term
        return 0

    acc[...] = jnp.zeros_like(acc)
    take(0)
    take(1)
    take_in(w_waits)
    for part in (wbuf.at[j_left, high], wbuf.at[j_right, low], wbuf.at[j_far]):
        to_sibling(part, part)
    sends_so_far = len(unsent)
    take(2)
    take_in(s_waits)
    lax.fori_loop(0, 3, lambda i, _: project(i - i // 2 * 3), 0)
    lax.fori_loop(0, 4, lambda i, _: project((2 + i // 2) * (1 - i % 2 * 2)), 0)
    for copy in unsent[:sends_so_far]:
        copy.wait_send()
    del unsent[:sends_so_far]

    def sent(i, _):
        tile_copy((ctx + i // GROUP) % CTX, (j + i) % GROUP).wait_send()
        return 0

    lax.fori_loop(1, PLANE, sent, 0)

    take(3)
    project(4)

    o_waits = []
    for i in range(1, GROUP):
        peer = (j + i) % GROUP
        rows = pl.ds(pl.multiple_of(peer * 64, 64), 64)
        osend[peer] = acc[rows, :].astype(bf16)
        o_waits.append(
            send(osend.at[peer], obuf.at[j], o_send.at[i], o_recv.at[i], at(ctx, z, peer))
        )
    obuf[j] = acc[pl.ds(pl.multiple_of(j * 64, 64), 64), :].astype(bf16)
    out_ref[:, pl.ds(pl.multiple_of(j * TOK, TOK), TOK)] = obuf[j]
    for i, copy in enumerate(o_waits):
        take_in([copy])
        source = (j + GROUP - 1 - i) % GROUP
        out_ref[:, pl.ds(pl.multiple_of(source * TOK, TOK), TOK)] = obuf[source]

    for copy in unsent:
        copy.wait_send()


def per_device(query_gate, key_gate, value_proj, filter_taps, out_weight):
    tokens = SEQ // CTX
    split = (CTX, CHAN, tokens)
    dma = pltpu.SemaphoreType.DMA
    return pl.pallas_call(
        layer_kernel,
        out_shape=jax.ShapeDtypeStruct((CTX * CHAN, tokens), bf16),
        in_specs=[pl.BlockSpec(memory_space=pl.ANY)] * 6,
        out_specs=pl.BlockSpec(memory_space=pltpu.VMEM),
        scratch_shapes=[
            pltpu.VMEM(split, bf16),
            pltpu.VMEM(split, bf16),
            pltpu.VMEM(split, bf16),
            pltpu.VMEM((CTX * CHAN, SEQ), bf16),
            pltpu.VMEM((END, 2 * N2), bf16),
            pltpu.VMEM((N1, 2 * N2), f32),
            pltpu.VMEM(split, bf16),
            pltpu.VMEM(split, bf16),
            pltpu.VMEM(split, bf16),
            pltpu.VMEM((N1 * CHAN, N2), f32),
            pltpu.VMEM((N1 * CHAN, N2), f32),
            pltpu.VMEM((N1 * CHAN, N2), f32),
            pltpu.VMEM((CHAN // BATCH, BATCH * N1, 2 * N2), f32),
            pltpu.VMEM((PLANE, CHAN, TOK), bf16),
            pltpu.VMEM((RING, PLANE, CHAN, TOK), bf16),
            pltpu.VMEM((GROUP, 64, D), bf16),
            pltpu.VMEM((SLAB, TOK), f32),
            pltpu.VMEM((GROUP, 64, TOK), bf16),
            pltpu.VMEM((GROUP, 64, TOK), bf16),
            dma((6,)),
            dma((CTX - 1,)), dma((CTX - 1,)), dma((CTX - 1,)), dma((CTX - 1,)),
            dma((6,)), dma((6,)), dma((6,)), dma((6,)),
            dma((PLANE,)), dma((PLANE,)),
            dma((4, 4)), dma((4, 4)), dma((4, 4)), dma((4, 4)),
            dma((GROUP,)), dma((GROUP,)),
        ],
        compiler_params=pltpu.CompilerParams(
            collective_id=0, has_side_effects=True, vmem_limit_bytes=54784 * 1024
        ),
    )(
        query_gate.reshape(split),
        key_gate.reshape(split),
        value_proj.reshape(split),
        filter_taps,
        out_weight.T,
        jnp.asarray(tables()),
    )


def solution(mesh):
    return jax.shard_map(
        per_device,
        mesh=mesh,
        in_specs=(P("ch", "ctx"), P("ch", "ctx"), P("ch", "ctx"), P("ch", None), P(None, "ch")),
        out_specs=P("ch", "ctx"),
        check_vma=False,
    )
```

```python
import jax
import jax.numpy as jnp
import ml_dtypes
import numpy as np
from jax import lax
from jax.experimental import pallas as pl
from jax.experimental.pallas import tpu as pltpu
from jax.sharding import PartitionSpec as P

SEQ = 8192
N1 = 64
N2 = 128
CTX = 4
GROUP = 8
CHAN = 16
BATCH = 16
RING = 8
PLANE = CTX * GROUP
TOK = 256
D = 4096
SLAB = D // RING
PART = PLANE // 4
NEAR = (0, 1, 3, 2)
MESH = pl.DeviceIdType.MESH

bf16 = jnp.bfloat16
f32 = jnp.float32


def two_parts(table):
    high = table.astype(ml_dtypes.bfloat16)
    low = (table - high.astype(np.float64)).astype(ml_dtypes.bfloat16)
    return high, low


def tables():
    root = np.pi / (2 * SEQ)
    n1, k1, n2, k2 = np.arange(N1), np.arange(N1), np.arange(N2), np.arange(N2)
    first = np.exp(1j * (root * N2 * n1[None, :] - 2 * np.pi * k1[:, None] * n1[None, :] / N1))
    twist = np.exp(1j * (root * n2[None, :] - 2 * np.pi * k1[:, None] * n2[None, :] / SEQ))
    second = np.exp(-2j * np.pi * n2[:, None] * k2[None, :] / N2)
    high, low = two_parts(np.concatenate([first.real, first.imag], axis=0))
    stage1 = np.concatenate([high, low], axis=1)
    fwd = two_parts(np.block([[second.real, second.imag], [-second.imag, second.real]]))
    inv = two_parts(np.block([[second.real, -second.imag], [second.imag, second.real]]))
    high, low = two_parts(np.concatenate([first.real.T, first.imag.T], axis=1) / SEQ)
    last = np.concatenate([high, low], axis=1)
    twist2 = two_parts(np.concatenate([twist.real, twist.imag], axis=1))
    stage1 = np.concatenate([stage1, np.zeros_like(stage1)], axis=1)
    return np.concatenate([*fwd, *inv, last, stage1, *twist2], axis=0)


FWD, INV, LAST, STAGE1, TWIST, END = np.cumsum([0, 4 * N2, 4 * N2, N1, 2 * N1, 2 * N1]).tolist()


def dot(a, b):
    return jnp.dot(a, b, preferred_element_type=f32)


def parts_of(x):
    high = x.astype(bf16)
    return high, (x - high.astype(f32)).astype(bf16)


def dot3(x, table_ref):
    high, low = parts_of(x)
    first, second = table_ref[: 2 * N2], table_ref[2 * N2 :]
    rows = x.shape[0]
    both = dot(jnp.concatenate([high, low], axis=0), first)
    return both[:rows] + (both[rows:] + dot(high, second))


def spectrum(ref, c0, stage1, tw_re, tw_im, fwd_ref):
    rows = []
    for c in range(BATCH):
        x = ref[pl.ds(c0 + c, N1, stride=CHAN), :].astype(bf16)
        a = dot(stage1, jnp.concatenate([x, x], axis=0))
        re, im = a[:N1], a[N1:]
        rows.append(jnp.concatenate([re * tw_re - im * tw_im, re * tw_im + im * tw_re], axis=1))
    return dot3(jnp.concatenate(rows, axis=0), fwd_ref)


def layer_kernel(
    q_in, k_in, v_in, f_in, w_in, table_in,
    out_ref,
    q_ref, k_ref, v_ref, f_ref, table, tw_ref,
    prod, pbuf, qbuf, sig, filt, conv, fspec, gsend, gbuf, wbuf, acc, osend, obuf,
    load_sem,
    p_send, p_recv, q_send, q_recv, w_send, w_recv, s_send, s_recv,
    g_send, g_recv, r_send, r_recv, l_send, l_recv, o_send, o_recv,
):
    ctx = lax.axis_index("ctx")
    ch = lax.axis_index("ch")
    z, j = ch // GROUP, ch % GROUP
    x, core = j // 2, j % 2
    me = ctx * GROUP + j

    def at(other_ctx, other_z, other_j):
        return (other_ctx, other_z * GROUP + other_j)

    def send(src, dst, send_sem, recv_sem, device):
        copy = pltpu.make_async_remote_copy(
            src_ref=src, dst_ref=dst, send_sem=send_sem, recv_sem=recv_sem,
            device_id=device, device_id_type=MESH,
        )
        copy.start()
        unsent.append(copy)
        unreceived.append(copy)
        return copy

    unsent, unreceived = [], []
    scattered = False

    def take_in(copies):
        for copy in copies:
            copy.wait_recv()
            unreceived[:] = [other for other in unreceived if other is not copy]

    up, down = at(ctx, (z + 1) % RING, j), at(ctx, (z + RING - 1) % RING, j)
    pairs = [
        (k_in, k_ref), (v_in, v_ref), (f_in, f_ref), (table_in, table), (q_in, q_ref),
        (w_in, wbuf.at[j]),
    ]
    loads = [
        pltpu.make_async_copy(src, dst, load_sem.at[i]) for i, (src, dst) in enumerate(pairs)
    ]
    for copy in loads:
        copy.start()
    barrier = pltpu.get_barrier_semaphore()

    def greet(i, _):
        peer = (me + 1 + (i + 12) % (PLANE - 1)) % PLANE
        pl.semaphore_signal(
            barrier, inc=1, device_id=at(peer // GROUP, z, peer % GROUP), device_id_type=MESH
        )
        return 0

    lax.fori_loop(0, PLANE - 1, greet, 0, unroll=True)
    pl.semaphore_signal(barrier, inc=1, device_id=up, device_id_type=MESH)
    pl.semaphore_signal(barrier, inc=1, device_id=down, device_id_type=MESH)

    loads[0].wait()
    loads[1].wait()
    prod[...] = (k_ref[...].astype(f32) * v_ref[...].astype(f32)).astype(bf16)
    pl.semaphore_wait(barrier, PLANE + 1)

    def spread(src, dst, send_sem, recv_sem):
        peers = [(ctx + i) % CTX for i in range(1, CTX)]
        return [
            send(src.at[peer], dst.at[ctx], send_sem.at[i], recv_sem.at[i], at(peer, z, j))
            for i, peer in enumerate(peers)
        ]

    p_waits = spread(prod, pbuf, p_send, p_recv)
    pbuf[ctx] = prod[ctx]

    xr, xl = (x + 1) % 4, (x + 3) % 4
    right, left = at(ctx, z, xr * 2 + core), at(ctx, z, xl * 2 + core)
    sibling = at(ctx, z, x * 2 + 1 - core)
    j_right, j_left, j_far = xr * 2 + core, xl * 2 + core, ((x + 2) % 4) * 2 + core
    low, high = pl.ds(0, 32), pl.ds(32, 32)

    def pass_weights(src, dst, i, device):
        return send(src, dst, w_send.at[i], w_recv.at[i], device)

    s_waits = []

    def to_sibling(src, dst):
        i = len(s_waits)
        s_waits.append(send(src, dst, s_send.at[i], s_recv.at[i], sibling))

    w_waits = [
        pass_weights(w_in.at[low], wbuf.at[j, low], 0, right),
        pass_weights(w_in.at[high], wbuf.at[j, high], 1, left),
    ]
    to_sibling(w_in, wbuf.at[j])

    for copy in loads[2:]:
        copy.wait()
    qbuf[ctx] = q_ref[ctx]

    own = pl.ds(pl.multiple_of(ctx * CHAN, CHAN), CHAN)

    def widen_filter(i, _):
        for k in range(CTX):
            n = k * 16 + i
            rows = pl.ds(pl.multiple_of(n * CHAN, CHAN), CHAN)
            filt[rows, :] = f_ref[own, pl.ds(pl.multiple_of(n * N2, N2), N2)].astype(f32)
        return 0

    lax.fori_loop(0, 16, widen_filter, 0)
    fwd_ref, inv_ref = table.at[FWD:INV], table.at[INV:LAST]
    stage1 = table[STAGE1:TWIST, : 2 * N1]
    twist = table[TWIST:END, :].astype(f32)
    tw_ref[...] = twist[:N1] + twist[N1:]
    tw_re, tw_im = tw_ref[:, :N2], tw_ref[:, N2:]

    def filter_step(i, _):
        fspec[i] = spectrum(filt, i * BATCH, stage1, tw_re, tw_im, fwd_ref)
        return 0

    lax.fori_loop(0, CHAN // BATCH, filter_step, 0)
    q_waits = spread(q_in, qbuf, q_send, q_recv)


    def widen_signal(i, part):
        for k in range(4):
            n = i * 4 + k
            rows = pl.ds(pl.multiple_of((part * 16 + n) * CHAN, CHAN), CHAN)
            sig[rows, :] = pbuf[part, :, pl.ds(pl.multiple_of(n * N2, N2), N2)].astype(f32)
        return part

    lax.fori_loop(0, 4, widen_signal, ctx)
    for i in (0, 2, 1):
        take_in([p_waits[i]])
        lax.fori_loop(0, 4, widen_signal, (ctx + CTX - 1 - i) % CTX)

    def conv_step(i, _):
        c0 = i * BATCH
        fs = fspec[i]
        ss = spectrum(sig, c0, stage1, tw_re, tw_im, fwd_ref)
        fr, fi, sr, si = fs[:, :N2], fs[:, N2:], ss[:, :N2], ss[:, N2:]
        back = dot3(jnp.concatenate([fr * sr - fi * si, fr * si + fi * sr], axis=1), inv_ref)
        last = table[LAST:STAGE1, :]
        for c in range(BATCH):
            re = back[c * N1 : (c + 1) * N1, :N2]
            im = back[c * N1 : (c + 1) * N1, N2:]
            u = jnp.concatenate([re * tw_re + im * tw_im, im * tw_re - re * tw_im], axis=0)
            high, low = parts_of(u)
            y = dot(last, jnp.concatenate([high, high], axis=0)) + dot(last[:, :N2], low)
            conv[pl.ds(c0 + c, N1, stride=CHAN), :] = y
        return 0

    lax.fori_loop(0, CHAN // BATCH, conv_step, 0)

    take_in(q_waits)
    slot = j * CTX + ctx

    def tile_copy(peer_ctx, peer_j):
        peer = peer_ctx * GROUP + peer_j
        return pltpu.make_async_remote_copy(
            src_ref=gsend.at[peer], dst_ref=gbuf.at[z, slot], send_sem=g_send.at[peer],
            recv_sem=g_recv.at[slot], device_id=at(peer_ctx, z, peer_j), device_id_type=MESH,
        )

    def gated_tile(peer_ctx, peer_j):
        halves = []
        for n in range(2):
            rows = pl.ds(pl.multiple_of((peer_ctx * 16 + peer_j * 2 + n) * CHAN, CHAN), CHAN)
            cols = pl.ds(pl.multiple_of(peer_j * TOK + n * N2, N2), N2)
            halves.append((qbuf[peer_ctx, :, cols].astype(f32) * conv[rows, :]).astype(bf16))
        return jnp.concatenate(halves, axis=1)

    def scatter(i, dx):
        peer_ctx, peer_j = (ctx + i // 2) % CTX, (x + dx) % 4 * 2 + (core + i) % 2
        gsend[peer_ctx * GROUP + peer_j] = gated_tile(peer_ctx, peer_j)
        tile_copy(peer_ctx, peer_j).start()
        return dx

    for dx in NEAR:
        lax.fori_loop(0 if dx else 1, PART, scatter, dx)
    gbuf[z, slot] = gated_tile(ctx, j)
    scattered = True

    def arrived(i, _):
        @pl.when(i != slot)
        def _():
            pltpu.make_async_remote_copy(
                src_ref=gsend.at[0], dst_ref=gbuf.at[z, i], send_sem=g_send.at[0],
                recv_sem=g_recv.at[i], device_id=up, device_id_type=MESH,
            ).wait_recv()

        return 0

    def pass_on(step, h):
        rows = pl.ds((x + 4 - NEAR[h]) % 4 * PART, PART)
        up_slab, down_slab = (z + RING - step) % RING, (z + step) % RING
        ups = downs = None
        if step < 3 or h < 2:
            part = gbuf.at[up_slab, rows]
            ups = send(part, part, r_send.at[step, h], r_recv.at[step, h], up)
        if step < 3 or h >= 2:
            part = gbuf.at[down_slab, rows]
            downs = send(part, part, l_send.at[step, h], l_recv.at[step, h], down)
        return ups, downs

    hops = {}
    for h in range(4):
        first = (x + 4 - NEAR[h]) % 4 * PART
        lax.fori_loop(first, first + PART, arrived, 0)
        hops[0, h] = pass_on(0, h)

    take_in(w_waits)
    from_left, from_right = wbuf.at[j_left, low], wbuf.at[j_right, high]
    w_waits = [
        pass_weights(from_left, from_left, 2, right),
        pass_weights(from_right, from_right, 3, left),
        pass_weights(w_in.at[high], wbuf.at[j, high], 4, right),
        pass_weights(w_in.at[low], wbuf.at[j, low], 5, left),
    ]
    to_sibling(from_left, from_left)
    to_sibling(from_right, from_right)

    def take(step):
        for h in range(4):
            ups, downs = hops[step, h]
            take_in([copy for copy in (ups, downs) if copy is not None])
            if step < 3:
                hops[step + 1, h] = pass_on(step + 1, h)

    def project(offset):
        slab = (z + RING + offset) % RING
        cols = pl.ds(pl.multiple_of(slab * SLAB, SLAB), SLAB)
        weight = wbuf[:, :, cols].reshape(SLAB, SLAB)
        term = dot(weight, gbuf[slab].reshape(SLAB, TOK))
        acc[...] += term
        return 0

    acc[...] = jnp.zeros_like(acc)
    take(0)
    take(1)
    take_in(w_waits)
    for part in (wbuf.at[j_left, high], wbuf.at[j_right, low], wbuf.at[j_far]):
        to_sibling(part, part)
    sends_so_far = len(unsent)
    take(2)
    take_in(s_waits)
    lax.fori_loop(0, 3, lambda i, _: project(i - i // 2 * 3), 0)
    lax.fori_loop(0, 4, lambda i, _: project((2 + i // 2) * (1 - i % 2 * 2)), 0)
    for copy in unsent[:sends_so_far]:
        copy.wait_send()
    del unsent[:sends_so_far]

    def sent(i, _):
        tile_copy((ctx + i // GROUP) % CTX, (j + i) % GROUP).wait_send()
        return 0

    lax.fori_loop(1, PLANE, sent, 0)

    take(3)
    project(4)

    o_waits = []
    for i in range(1, GROUP):
        peer = (j + i) % GROUP
        rows = pl.ds(pl.multiple_of(peer * 64, 64), 64)
        osend[peer] = acc[rows, :].astype(bf16)
        o_waits.append(
            send(osend.at[peer], obuf.at[j], o_send.at[i], o_recv.at[i], at(ctx, z, peer))
        )
    obuf[j] = acc[pl.ds(pl.multiple_of(j * 64, 64), 64), :].astype(bf16)
    out_ref[:, pl.ds(pl.multiple_of(j * TOK, TOK), TOK)] = obuf[j]
    for i, copy in enumerate(o_waits):
        take_in([copy])
        source = (j + GROUP - 1 - i) % GROUP
        out_ref[:, pl.ds(pl.multiple_of(source * TOK, TOK), TOK)] = obuf[source]

    for copy in unsent:
        copy.wait_send()


def per_device(query_gate, key_gate, value_proj, filter_taps, out_weight):
    tokens = SEQ // CTX
    split = (CTX, CHAN, tokens)
    dma = pltpu.SemaphoreType.DMA
    return pl.pallas_call(
        layer_kernel,
        out_shape=jax.ShapeDtypeStruct((CTX * CHAN, tokens), bf16),
        in_specs=[pl.BlockSpec(memory_space=pl.ANY)] * 6,
        out_specs=pl.BlockSpec(memory_space=pltpu.VMEM),
        scratch_shapes=[
            pltpu.VMEM(split, bf16),
            pltpu.VMEM(split, bf16),
            pltpu.VMEM(split, bf16),
            pltpu.VMEM((CTX * CHAN, SEQ), bf16),
            pltpu.VMEM((END, 2 * N2), bf16),
            pltpu.VMEM((N1, 2 * N2), f32),
            pltpu.VMEM(split, bf16),
            pltpu.VMEM(split, bf16),
            pltpu.VMEM(split, bf16),
            pltpu.VMEM((N1 * CHAN, N2), f32),
            pltpu.VMEM((N1 * CHAN, N2), f32),
            pltpu.VMEM((N1 * CHAN, N2), f32),
            pltpu.VMEM((CHAN // BATCH, BATCH * N1, 2 * N2), f32),
            pltpu.VMEM((PLANE, CHAN, TOK), bf16),
            pltpu.VMEM((RING, PLANE, CHAN, TOK), bf16),
            pltpu.VMEM((GROUP, 64, D), bf16),
            pltpu.VMEM((SLAB, TOK), f32),
            pltpu.VMEM((GROUP, 64, TOK), bf16),
            pltpu.VMEM((GROUP, 64, TOK), bf16),
            dma((6,)),
            dma((CTX - 1,)), dma((CTX - 1,)), dma((CTX - 1,)), dma((CTX - 1,)),
            dma((6,)), dma((6,)), dma((6,)), dma((6,)),
            dma((PLANE,)), dma((PLANE,)),
            dma((4, 4)), dma((4, 4)), dma((4, 4)), dma((4, 4)),
            dma((GROUP,)), dma((GROUP,)),
        ],
        compiler_params=pltpu.CompilerParams(
            collective_id=0, has_side_effects=True, vmem_limit_bytes=54784 * 1024
        ),
    )(
        query_gate.reshape(split),
        key_gate.reshape(split),
        value_proj.reshape(split),
        filter_taps,
        out_weight.T,
        jnp.asarray(tables()),
    )


def solution(mesh):
    return jax.shard_map(
        per_device,
        mesh=mesh,
        in_specs=(P("ch", "ctx"), P("ch", "ctx"), P("ch", "ctx"), P("ch", None), P(None, "ch")),
        out_specs=P("ch", "ctx"),
        check_vma=False,
    )
```
